128 devices in a mesh: seq: 32 (over z, y, core), batch: 4 (over x).
Axes of the slice: x: 4, y: 4, z: 4, core: 2. Of those that a mesh axis runs over, the one named last changes fastest.
Arguments:
- tokens: bfloat16 [4, 4096, 1408], P('batch', 'seq')
- qkv_weight: bfloat16 [1408, 4224], P('batch'), may hold values from -0.15625 to 0.15625
- out_weight: bfloat16 [1408, 1408], P('batch'), may hold values from -0.15625 to 0.15625
- mask_blocks: int32 [4, 56], replicated, may hold values from 0 to 63, as said below
- owner_map: int32 [4, 64], replicated, may hold values from 0 to 3, as said below
- pred_stream: bfloat16 [4, 4, 4096, 384], P('batch', None, 'seq'), may hold values from -6 to 6
- pred_up: bfloat16 [384, 1536], replicated, may hold values from -0.3125 to 0.3125
- pred_down: bfloat16 [1536, 384], replicated, may hold values from -0.15625 to 0.15625
- pred_proj: bfloat16 [384, 1408], replicated, may hold values from -0.3125 to 0.3125
Outputs:
- grad_up: float32 [384, 1536], P(None, ('seq', 'batch'))
- grad_down: float32 [1536, 384], P(('seq', 'batch'))
The draws below stay inside these ranges and needn't reach their ends.
Inputs may be any that keep to these rules, and one draw needn't show every extreme that they name: `mask_blocks`: the 56 entries of one clip are distinct block indices; each aligned group of 2 blocks (those of one device) holds 2 or 1 of them. `owner_map`: within one clip, the blocks of one aligned group of 2 have distinct owners.
All inputs are finite; a program needn't handle non-finite values.
Results may differ from the reference program's by a relative error of at most 0.005.
Values may be sent and summed in bfloat16 or wider, within the bound.
A program may use at most 128 MiB of HBM per device.

```python
import jax
import jax.numpy as jnp
from jax import lax

D = 1408
H = 16
HD = 88
PD = 384
PH = 1536
BLK = 64
BLK_DEV = 2
TOKENS = 4096
BLOCKS = 64
MASK_BLK = 56
BATCH = 4


pattern_count = 32


def joint_draw(key):
    base = jax.random.fold_in(key, 29)
    groups = BLOCKS // BLK_DEV
    key_star, key_owner, key_clips = jax.random.split(base, 3)
    star_group = jax.random.randint(key_star, (), 0, groups)
    star_owner = jax.random.randint(key_owner, (), 0, BATCH).astype(jnp.int32)
    position = jnp.arange(BLK_DEV, dtype=jnp.int32)

    def one_clip(clip_key):
        key_a, key_b, key_c, key_d = jax.random.split(clip_key, 4)
        order = jax.random.permutation(key_a, groups)
        single = jnp.zeros((groups,), jnp.int32).at[order[:groups // 4]].set(1)
        dropped = jax.random.randint(key_b, (groups,), 0, BLK_DEV)
        masked = 1 - single[:, None] * (position[None, :] == dropped[:, None]).astype(jnp.int32)
        owner_keys = jax.random.split(key_c, groups)
        rows = jax.vmap(lambda one_key: jax.random.permutation(one_key, BATCH)[:BLK_DEV])(owner_keys).astype(jnp.int32)
        first = jnp.where(masked[:, 0] == 1, 0, 1).astype(jnp.int32)
        at_first = jnp.take_along_axis(rows, first[:, None], axis=1)
        swapped = jnp.where(rows == star_owner, at_first, rows)
        forced = jnp.where(position[None, :] == first[:, None], star_owner, swapped)
        is_star = (jnp.arange(groups) == star_group)[:, None]
        owners = jnp.where(is_star, forced, rows).reshape(BLOCKS).astype(jnp.int32)
        flat_masked = masked.reshape(BLOCKS)
        ranks = jax.random.permutation(key_d, BLOCKS).astype(jnp.int32)
        score = jnp.where(flat_masked == 1, ranks, BLOCKS + jnp.arange(BLOCKS, dtype=jnp.int32))
        picked = jnp.argsort(score, stable=True)[:MASK_BLK].astype(jnp.int32)
        return (picked, owners)
    clip_keys = jax.random.split(key_clips, BATCH)
    return jax.vmap(one_clip)(clip_keys)


def draw_mask_blocks(key, part):
    return joint_draw(key)[0].astype(jnp.int32)


def draw_owner_map(key, part):
    return joint_draw(key)[1].astype(jnp.int32)


def draw_tokens(key, part):
    key_common, key_noise, key_assign = jax.random.split(jax.random.fold_in(key, 41), 3)
    common = jax.random.normal(key_common, (BATCH, pattern_count, D), jnp.float32)
    assign = jax.random.randint(key_assign, (BATCH, TOKENS), 0, pattern_count).astype(jnp.int32)
    spread = jax.vmap(lambda table, which: table[which])(common, assign)
    noise = jax.random.normal(key_noise, (BATCH, TOKENS, D), jnp.float32)
    scales = jnp.ones((BATCH, TOKENS, 1), jnp.float32)
    values = 0.1 * scales * (spread + 0.5 * noise)
    return values.astype(jnp.bfloat16)


def block_scale(stream_key, extent, cuts, smallest, largest):
    def one(dim, shards_of):
        steps = jax.random.uniform(jax.random.fold_in(jax.random.fold_in(stream_key, 6), dim), (shards_of,), jnp.float32, smallest / len(cuts), largest / len(cuts))
        return jnp.repeat(jnp.exp(steps), extent[dim] // shards_of).reshape((-1,) + (1,) * (len(extent) - dim - 1))

    level = one(*cuts[0])
    for cut in cuts[1:]:
        level = level * one(*cut)
    return level


def scatter_about(key, extent, scale, bound, pieces=(), kind=jnp.bfloat16):
    values = scale * jax.random.normal(key, extent, jnp.float32)
    if pieces:
        values = values * block_scale(key, extent, pieces, -0.22, 0.18)
    return jnp.clip(values, -bound, bound).astype(kind)


def setup_inputs(seed: int = 0) -> dict:
    key_list = jax.random.split(jax.random.key(seed), 10)
    return {
        "tokens": draw_tokens(jax.random.fold_in(key_list[9], 71), 0),
        "qkv_weight": scatter_about(key_list[1], (D, 3 * D), D ** -0.5, 0.15625, ((0, 4),)),
        "out_weight": scatter_about(key_list[2], (D, D), D ** -0.5, 0.15625, ((0, 4),)),
        "mask_blocks": draw_mask_blocks(jax.random.fold_in(key_list[9], 71), 0),
        "owner_map": draw_owner_map(jax.random.fold_in(key_list[9], 71), 0),
        "pred_stream": scatter_about(key_list[5], (BATCH, BATCH, TOKENS, PD), 1.0, 6.0, ((0, 4), (2, 32))),
        "pred_up": scatter_about(key_list[6], (PD, PH), PD ** -0.5, 0.3125),
        "pred_down": scatter_about(key_list[7], (PH, PD), PH ** -0.5, 0.15625),
        "pred_proj": scatter_about(key_list[8], (PD, D), PD ** -0.5, 0.3125),
    }


gelu_coef = 0.7978845608
gelu_cube = 0.044715

def layer_norm(values):
    center = values - lax.optimization_barrier(jnp.mean(values, axis=-1, keepdims=True))
    variance = lax.optimization_barrier(jnp.mean(center * center, axis=-1, keepdims=True))
    factor = lax.rsqrt(variance + 1e-06)
    return (center * factor, factor)

def gelu_tanh(values):
    inner = gelu_coef * (values + gelu_cube * values * values * values)
    return 0.5 * values * (1.0 + jnp.tanh(inner))

def gelu_slope(values):
    inner = gelu_coef * (values + gelu_cube * values * values * values)
    tangent = jnp.tanh(inner)
    return 0.5 * (1.0 + tangent) + 0.5 * values * (1.0 - tangent * tangent) * gelu_coef * (1.0 + 3.0 * gelu_cube * values * values)

def predictor_grads(stream, target_rows, live_rows, pred_up, pred_down, pred_proj, divisor):
    stream_f = stream.astype(jnp.float32)
    normed_pred = layer_norm(stream_f)[0].astype(jnp.bfloat16)
    hidden_pre = jnp.dot(normed_pred, pred_up, preferred_element_type=jnp.float32)
    hidden = gelu_tanh(hidden_pre).astype(jnp.bfloat16)
    mixed = stream_f + jnp.dot(hidden, pred_down, preferred_element_type=jnp.float32)
    mixed_norm, rstd = layer_norm(mixed)
    mixed_rounded = mixed_norm.astype(jnp.bfloat16)
    prediction = jnp.dot(mixed_rounded, pred_proj, preferred_element_type=jnp.float32)
    error = (prediction - target_rows.astype(jnp.float32)) * live_rows[:, None]
    grad_pred = (error / divisor).astype(jnp.bfloat16)
    grad_norm = jnp.dot(grad_pred, pred_proj.T, preferred_element_type=jnp.float32)
    first_mean = lax.optimization_barrier(jnp.mean(grad_norm, axis=-1, keepdims=True))
    second_mean = lax.optimization_barrier(jnp.mean(grad_norm * mixed_norm, axis=-1, keepdims=True))
    grad_mixed = (rstd * (grad_norm - first_mean - mixed_norm * second_mean)).astype(jnp.bfloat16)
    grad_down = jnp.dot(hidden.T, grad_mixed, preferred_element_type=jnp.float32)
    grad_hidden = jnp.dot(grad_mixed, pred_down.T, preferred_element_type=jnp.float32)
    grad_pre = (grad_hidden * gelu_slope(hidden_pre)).astype(jnp.bfloat16)
    grad_up = jnp.dot(normed_pred.T, grad_pre, preferred_element_type=jnp.float32)
    return (grad_up, grad_down)

def encode(clip_tokens, qkv_weight, out_weight):
    stream_f = clip_tokens.astype(jnp.float32)
    normed = layer_norm(stream_f)[0].astype(jnp.bfloat16)
    projected = jnp.dot(normed, qkv_weight, preferred_element_type=jnp.float32).astype(jnp.bfloat16)
    queries = projected[:, :D].reshape(TOKENS, H, HD).transpose(1, 0, 2)
    keys = projected[:, D:2 * D].reshape(TOKENS, H, HD).transpose(1, 0, 2)
    values = projected[:, 2 * D:].reshape(TOKENS, H, HD).transpose(1, 0, 2)
    scale = 1.0 / HD ** 0.5

    def one_head(inputs):
        head_q, head_k, head_v = inputs
        scores = jnp.dot(head_q, head_k.T, preferred_element_type=jnp.float32) * scale
        weights = jnp.exp(scores)
        totals = lax.optimization_barrier(jnp.sum(weights, axis=1))
        summed = jnp.dot(weights.astype(jnp.bfloat16), head_v, preferred_element_type=jnp.float32)
        return summed / totals[:, None]
    heads_out = lax.map(one_head, (queries, keys, values))
    attended = heads_out.transpose(1, 0, 2).reshape(TOKENS, D).astype(jnp.bfloat16)
    summed = stream_f + jnp.dot(attended, out_weight, preferred_element_type=jnp.float32)
    return layer_norm(summed)[0].astype(jnp.bfloat16)

def reference(tokens, qkv_weight, out_weight, mask_blocks, owner_map, pred_stream, pred_up, pred_down, pred_proj):
    target = lax.map(lambda clip_tokens: encode(clip_tokens, qkv_weight, out_weight), tokens)
    block_index = jnp.arange(BLOCKS, dtype=jnp.int32)
    masked = jnp.any(mask_blocks[:, :, None] == block_index[None, None, :], axis=1)
    token_block = jnp.arange(TOKENS, dtype=jnp.int32) // BLK
    live_tok = masked[:, token_block].astype(jnp.float32)
    owner_tok = owner_map[:, token_block].astype(jnp.int32)
    picked = jnp.take_along_axis(pred_stream, owner_tok[None, :, :, None], axis=0)[0]
    divisor = float(BATCH * MASK_BLK)
    return predictor_grads(picked.reshape(BATCH * TOKENS, PD), target.reshape(BATCH * TOKENS, D), live_tok.reshape(BATCH * TOKENS), pred_up, pred_down, pred_proj, divisor)
```

```python
import functools

import jax
import jax.numpy as jnp
from jax import lax
from jax.experimental import pallas as pl
from jax.experimental.pallas import tpu as pltpu
from jax.sharding import PartitionSpec as P

MESH = pl.DeviceIdType.MESH
BF = jnp.bfloat16
F32 = jnp.float32

D = 1408
H = 16
HD = 88
PD = 384
PH = 1536
BLK = 64
ROWS = 128
GRP = 384
HS = 256
LOG2E = 1.4426950408889634
NT = (((1,), (1,)), ((), ()))
TN = (((0,), (0,)), ((), ()))

gelu_coef = 0.7978845608
gelu_cube = 0.044715


def mm(a, b, dims=(((1,), (0,)), ((), ()))):
    return lax.dot_general(a, b, dims, preferred_element_type=F32)


def layer_norm(values):
    center = values - jnp.mean(values, axis=-1, keepdims=True)
    variance = jnp.mean(center * center, axis=-1, keepdims=True)
    factor = lax.rsqrt(variance + 1e-06)
    return center * factor, factor


def gelu_parts(values):
    inner = gelu_coef * (values + gelu_cube * values * values * values)
    tangent = jnp.tanh(inner)
    value = 0.5 * values * (1.0 + tangent)
    slope = 0.5 * (1.0 + tangent) + 0.5 * values * (1.0 - tangent * tangent) * gelu_coef * (
        1.0 + 3.0 * gelu_cube * values * values
    )
    return value, slope


class Here:
    def __init__(self):
        self.seq = lax.axis_index("seq")
        self.x = lax.axis_index("batch")
        self.k = lax.rem(self.seq, 2)
        self.y = lax.rem(lax.div(self.seq, 2), 4)
        self.z = lax.div(self.seq, 8)

    def at(self, x=None, y=None, z=None, k=None):
        x = self.x if x is None else x
        y = self.y if y is None else y
        z = self.z if z is None else z
        k = self.k if k is None else k
        return {"seq": (z * 4 + y) * 2 + k, "batch": x}

    def step(self, axis, by):
        pos = lax.rem(getattr(self, axis) + by, 4)
        return pos, self.at(**{axis: pos})

    def partner(self):
        return self.at(k=1 - self.k)


class Net:
    def __init__(self, send, recv):
        self.send, self.recv, self.n = send, recv, 0

    def copy(self, src, dst, dev):
        i = self.n
        self.n += 1
        return pltpu.make_async_remote_copy(
            src_ref=src, dst_ref=dst, send_sem=self.send.at[i], recv_sem=self.recv.at[i],
            device_id=dev, device_id_type=MESH,
        )


def greet(devices):
    barrier = pltpu.get_barrier_semaphore()
    for dev in devices:
        pl.semaphore_signal(barrier, inc=1, device_id=dev, device_id_type=MESH)
    pl.semaphore_wait(barrier, len(devices))


class RingGather:
    def __init__(self, net, here, axis, own, buf, stride, base, rows_a, rows):
        self.net, self.buf = net, buf
        self.stride, self.base, self.ra, self.rows = stride, base, rows_a, rows
        self.me = getattr(here, axis)
        self.right_pos, self.right = here.step(axis, 1)
        self.left_pos, self.left = here.step(axis, 3)
        self.far_pos, _ = here.step(axis, 2)
        rb = rows - rows_a
        a, b = pl.ds(0, rows_a), pl.ds(rows_a, rb)
        self.ra_c = net.copy(own.at[a], self.part(self.me, 0), self.right)
        self.lb_c = net.copy(own.at[b], self.part(self.me, 1), self.left)
        self.rb_c = net.copy(own.at[b], self.part(self.me, 1), self.right)
        self.la_c = net.copy(own.at[a], self.part(self.me, 0), self.left)
        self.fa_c = net.copy(self.part(self.left_pos, 0), self.part(self.left_pos, 0), self.right)
        self.fb_c = net.copy(self.part(self.right_pos, 1), self.part(self.right_pos, 1), self.left)

    def offset(self, pos, part):
        off = pos * self.stride + self.base + (self.ra if part == 1 else 0)
        return pl.multiple_of(off, 16)

    def part(self, pos, part):
        n = self.ra if part == 0 else self.rows - self.ra
        return self.buf.at[pl.ds(self.offset(pos, part), n)]

    def whole(self, pos):
        return self.buf.at[pl.ds(self.offset(pos, 0), self.rows)]

    def start(self):
        for c in (self.ra_c, self.lb_c, self.rb_c, self.la_c):
            c.start()

    def forward(self):
        self.ra_c.wait_recv()
        self.fa_c.start()
        self.lb_c.wait_recv()
        self.fb_c.start()

    def near(self):
        self.rb_c.wait_recv()
        self.la_c.wait_recv()

    def far(self):
        self.fa_c.wait_recv()
        self.fb_c.wait_recv()

    def drain(self):
        for c in (self.ra_c, self.lb_c, self.rb_c, self.la_c, self.fa_c, self.fb_c):
            c.wait_send()


class Mirror:
    def __init__(self, net, here, gather, own):
        self.copies = []
        dev = here.partner()
        if own is not None:
            self.copies.append(net.copy(own, gather.whole(gather.me), dev))
        for pos in (gather.left_pos, gather.right_pos, gather.far_pos):
            w = gather.whole(pos)
            self.copies.append(net.copy(w, w, dev))

    def start(self, which):
        for i in which:
            self.copies[i].start()

    def wait_recv(self):
        for c in self.copies:
            c.wait_recv()

    def drain(self):
        for c in self.copies:
            c.wait_send()


def spread(rows, cols):
    i = lax.broadcasted_iota(jnp.int32, (rows, cols), 0)
    j = lax.broadcasted_iota(jnp.int32, (rows, cols), 1)
    lane = j % 128
    return jnp.where((lane < HD) & (i == (j // 128) * HD + lane), 1.0, 0.0).astype(BF)


def gather_spread(rows, cols):
    i = lax.broadcasted_iota(jnp.int32, (rows, cols), 0)
    j = lax.broadcasted_iota(jnp.int32, (rows, cols), 1)
    lane = i % 128
    return jnp.where((lane < HD) & (j == (i // 128) * HD + lane), 1.0, 0.0).astype(BF)


def qkv_kernel(
    tok_ref, wgrp_ref, spick_ref, up_ref, down_ref, proj_ref, owner_ref,
    qkv_ref, kvp_ref, pred_ref, mnorm_ref, rstd_ref, nall_ref, hid_ref, slope_ref, pds_ref,
    tokbuf, normed, wbuf, sbuf, outq, bounce, send, recv, local,
):
    here = Here()
    net = Net(send, recv)
    peers = [here.step(a, s)[1] for a in ("x", "y", "z") for s in (1, 3)] + [here.partner()]
    greet(peers)

    gs = RingGather(net, here, "x", spick_ref, sbuf.at[here.k], 256, 0, 128, 256)
    gt = RingGather(net, here, "y", tok_ref, tokbuf, 128, 0, 64, 128)
    gw = RingGather(
        net, here, "x", wgrp_ref.at[pl.ds(pl.multiple_of(176 * here.k, 16), 176)],
        wbuf, 352, 176 * here.k, 96, 176,
    )
    ms = Mirror(net, here, gs, spick_ref)
    mw = Mirror(net, here, gw, None)
    gt.start()
    gw.start()
    gs.start()
    ms.start([0])
    own_w = pltpu.make_async_copy(
        wgrp_ref, wbuf.at[pl.ds(pl.multiple_of(352 * here.x, 16), 352)], local.at[0]
    )
    own_w.start()
    own_s = pltpu.make_async_copy(spick_ref, gs.whole(here.x), local.at[1])
    own_s.start()

    def norm_block(src, pos):
        value = layer_norm(src.astype(F32))[0].astype(BF)
        normed[pl.ds(pl.multiple_of(pos * 128, 128), 128), :] = value

    norm_block(tok_ref[...], here.y)
    i = lax.broadcasted_iota(jnp.int32, (PH, HS), 0)
    j = lax.broadcasted_iota(jnp.int32, (PH, HS), 1)
    unit = ((j // 16) * 2 + here.k) * 48 + here.x * 12 + j % 16
    select = jnp.where((j % 16 < 12) & (i == unit), 1.0, 0.0).astype(BF)
    ups = mm(up_ref[...], select).astype(BF)
    pds_ref[...] = mm(select, down_ref[...], TN).astype(BF)

    gt.forward()
    gw.forward()
    gt.near()
    for pos in (gt.left_pos, gt.right_pos):
        norm_block(gt.whole(pos)[...], pos)
    gs.forward()
    gw.near()
    mw.start([0, 1])
    gs.near()
    ms.start([1, 2])
    gt.far()
    norm_block(gt.whole(gt.far_pos)[...], gt.far_pos)
    gw.far()
    mw.start([2])
    gs.far()
    ms.start([3])
    own_w.wait()
    mw.wait_recv()

    pad = spread(GRP, 512)
    lane = lax.broadcasted_iota(jnp.int32, (1, 512), 1) % 128
    ones = jnp.where(lane >= HD, 1.0, 0.0)
    for t in range(3):
        part = mm(normed[...], wbuf[:, t * GRP:(t + 1) * GRP])
        if t == 0:
            part = part * (LOG2E / HD**0.5)
        wide = mm(part.astype(BF), pad)
        if t == 2:
            wide = wide + ones
        wide = wide.astype(BF)
        for h in range(4):
            outq[h, :, t * 128:(t + 1) * 128] = wide[:, h * 128:(h + 1) * 128]

    zr, right = here.step("z", 1)
    zl, left = here.step("z", 3)
    zf, _ = here.step("z", 2)
    a, b = pl.ds(0, 256), pl.ds(256, 256)
    far_a = net.copy(outq.at[zf, a], bounce.at[0], right)
    far_b = net.copy(outq.at[zf, b], bounce.at[1], left)
    to_r = net.copy(outq.at[zr], qkv_ref.at[here.z], right)
    to_l = net.copy(outq.at[zl], qkv_ref.at[here.z], left)
    for c in (far_a, far_b, to_r, to_l):
        c.start()
    own_q = pltpu.make_async_copy(outq.at[here.z], qkv_ref.at[here.z], local.at[2])
    own_q.start()
    kv_own = net.copy(
        outq.at[here.z, :, pl.ds(128, 256)], kvp_ref.at[here.z], here.partner()
    )
    kv_own.start()

    own_s.wait()
    ms.wait_recv()

    def rows_of(c, k):
        blocks = [sbuf[k, pl.ds(owner_ref[c, k, b] * 256 + c * 64, 64), :] for b in range(2)]
        return jnp.concatenate(blocks, axis=0)

    blocks = [
        sbuf[here.k, pl.ds(owner_ref[4, here.k, b] * 256 + here.x * 64, 64), :] for b in range(2)
    ]
    stream = jnp.concatenate(blocks, axis=0).astype(F32)
    normed_own = layer_norm(stream)[0].astype(BF)
    hidden = gelu_parts(mm(normed_own, up_ref[...]))[0].astype(BF)
    mixed = stream + mm(hidden, down_ref[...])
    mixed_norm, rstd = layer_norm(mixed)
    mnorm_ref[...] = mixed_norm
    rstd_ref[...] = rstd
    pred_ref[...] = mm(mixed_norm.astype(BF), proj_ref[...])

    far_a.wait_recv()
    fwd_a = net.copy(bounce.at[0], qkv_ref.at[zl, a], right)
    fwd_a.start()
    far_b.wait_recv()
    fwd_b = net.copy(bounce.at[1], qkv_ref.at[zr, b], left)
    fwd_b.start()

    for c in range(4):
        for k in range(2):
            at = pl.ds((c * 2 + k) * 128, 128)
            nv = layer_norm(rows_of(c, k).astype(F32))[0].astype(BF)
            nall_ref[at, :] = nv
            value, slope = gelu_parts(mm(nv, ups))
            hid_ref[at, :] = value.astype(BF)
            slope_ref[at, :] = slope

    to_r.wait_recv()
    kv_l = net.copy(qkv_ref.at[zl, :, pl.ds(128, 256)], kvp_ref.at[zl], here.partner())
    kv_l.start()
    to_l.wait_recv()
    kv_r = net.copy(qkv_ref.at[zr, :, pl.ds(128, 256)], kvp_ref.at[zr], here.partner())
    kv_r.start()
    fwd_a.wait_recv()
    fwd_b.wait_recv()
    kv_f = net.copy(qkv_ref.at[zf, :, pl.ds(128, 256)], kvp_ref.at[zf], here.partner())
    kv_f.start()
    for c in (kv_own, kv_l, kv_r, kv_f):
        c.wait_recv()
    own_q.wait()
    for c in (gs, gt, gw, ms, mw):
        c.drain()
    for c in (far_a, far_b, to_r, to_l, kv_own, fwd_a, fwd_b, kv_l, kv_r, kv_f):
        c.wait_send()


def attend_kernel(
    qkv_ref, kvp_ref, ow_ref, att_ref, wout_ref, atts, send, recv, asend, arecv, local
):
    here = Here()
    net = Net(send, recv)
    peers = [here.step("x", s)[1] for s in (1, 3)] + [here.partner()]
    for dz in range(4):
        for dy in range(4):
            if dz or dy:
                peers.append(here.at(z=lax.rem(here.z + dz, 4), y=lax.rem(here.y + dy, 4)))
    greet(peers)
    gw = RingGather(
        net, here, "x", ow_ref.at[pl.ds(pl.multiple_of(176 * here.k, 16), 176)],
        wout_ref, 352, 176 * here.k, 96, 176,
    )
    mw = Mirror(net, here, gw, None)
    gw.start()
    own_w = pltpu.make_async_copy(
        ow_ref, wout_ref.at[pl.ds(pl.multiple_of(352 * here.x, 16), 352)], local.at[0]
    )
    own_w.start()
    wout_ref[pl.ds(D, 32), :] = jnp.zeros((32, D), BF)
    head = here.y * 4 + here.z

    def back(i, j):
        zc = lax.rem(here.z + 1 + i, 4)
        yc = lax.rem(here.y + 1 + j, 4)
        slot = i * 4 + j
        return pltpu.make_async_remote_copy(
            src_ref=atts.at[slot], dst_ref=att_ref.at[head],
            send_sem=asend.at[slot], recv_sem=arecv.at[head],
            device_id=here.at(z=zc, y=yc), device_id_type=MESH,
        )

    def run(i):
        zc = lax.rem(here.z + 1 + i, 4)
        acc_of(i, zc)
        for j in range(4):
            if isinstance(i, int) and i == 3 and j == 3:
                continue
            back(i, j).start()

    def acc_of(i, zc):
        for half in range(2):
            q = qkv_ref[zc, half * 256:(half + 1) * 256, 0:128]
            acc = jnp.zeros((256, 128), F32)
            for t in range(4):
                for own in (0, 1):
                    if own:
                        key, val = qkv_ref[t, :, 128:256], qkv_ref[t, :, 256:384]
                    else:
                        key, val = kvp_ref[t, :, 0:128], kvp_ref[t, :, 128:256]
                    p = jnp.exp2(mm(q, key, NT)).astype(BF)
                    acc = acc + mm(p, val)
            out = (acc / acc[:, HD:HD + 1]).astype(BF)
            for w in range(2):
                yc = half * 2 + w
                j = lax.rem(yc - here.y + 7, 4)
                atts[i * 4 + j] = out[w * 128:(w + 1) * 128]

    @pl.loop(0, 2)
    def _(i):
        run(i)

    gw.forward()
    run(2)
    gw.near()
    mw.start([0, 1])
    gw.far()
    mw.start([2])
    run(3)
    own = pltpu.make_async_copy(atts.at[15], att_ref.at[head], local.at[1])
    own.start()
    own.wait()
    own_w.wait()
    mw.wait_recv()
    gw.drain()
    mw.drain()
    for slot in range(15):
        back(slot // 4, slot % 4).wait_send()
    for d in range(1, 16):
        src = lax.rem(head + d, 16)
        pltpu.make_async_remote_copy(
            src_ref=atts.at[0], dst_ref=att_ref.at[src],
            send_sem=asend.at[0], recv_sem=arecv.at[src],
            device_id=here.partner(), device_id_type=MESH,
        ).wait_recv()


def grads_kernel(
    att_ref, wout_ref, tok_ref, live_ref, pred_ref, mnorm_ref, rstd_ref, nall_ref, hid_ref,
    slope_ref, pds_ref, proj_ref, out_ref, gm, gmall, part, land, send, recv, asend, arecv, local,
):
    here = Here()
    net = Net(send, recv)
    peers = [here.step("x", s)[1] for s in (1, 3)] + [here.partner()]
    for dz in range(4):
        for dy in range(4):
            if dz or dy:
                peers.append(here.at(z=lax.rem(here.z + dz, 4), y=lax.rem(here.y + dy, 4)))
    greet(peers)

    pack = gather_spread(512, GRP)
    total = tok_ref[...].astype(F32)
    for x in range(4):
        wide = jnp.concatenate([att_ref[4 * x + h] for h in range(4)], axis=1)
        total = total + mm(mm(wide, pack).astype(BF), wout_ref[352 * x:352 * x + GRP, :])
    target = layer_norm(total)[0].astype(BF).astype(F32)
    grad_pred = ((pred_ref[...] - target) * live_ref[...]).astype(BF)
    grad_norm = mm(grad_pred, proj_ref[...], NT)
    mixed_norm = mnorm_ref[...]
    first_mean = jnp.mean(grad_norm, axis=-1, keepdims=True)
    second_mean = jnp.mean(grad_norm * mixed_norm, axis=-1, keepdims=True)
    gm[...] = (rstd_ref[...] * (grad_norm - first_mean - mixed_norm * second_mean)).astype(BF)

    gg = RingGather(net, here, "x", gm, gmall.at[here.k], 128, 0, 64, 128)
    mg = Mirror(net, here, gg, gm)
    gg.start()
    mg.start([0])
    own = pltpu.make_async_copy(gm, gg.whole(here.x), local.at[0])
    own.start()
    gg.forward()
    gg.near()
    mg.start([1, 2])
    gg.far()
    mg.start([3])
    own.wait()
    mg.wait_recv()

    rows = [gmall[k, c * 128:(c + 1) * 128, :] for c in range(4) for k in range(2)]
    grad_mixed = jnp.concatenate(rows, axis=0)
    grad_down = mm(hid_ref[...], grad_mixed, TN)
    grad_hidden = mm(grad_mixed, pds_ref[...], NT)
    grad_pre = (grad_hidden * slope_ref[...]).astype(BF)
    grad_up = mm(grad_pre, nall_ref[...], TN)
    part[:, :, 0:PD] = grad_up.astype(BF).reshape(16, 16, PD)
    part[:, :, PD:2 * PD] = grad_down.astype(BF).reshape(16, 16, PD)

    me = here.z * 4 + here.y
    copies = []
    for d in range(1, 16):
        to = lax.rem(me + d, 16)
        copies.append(
            pltpu.make_async_remote_copy(
                src_ref=part.at[to], dst_ref=land.at[me],
                send_sem=asend.at[d], recv_sem=arecv.at[me],
                device_id=here.at(z=lax.div(to, 4), y=lax.rem(to, 4)), device_id_type=MESH,
            )
        )
        copies[-1].start()
    total = part[me].astype(F32)
    for d in range(1, 16):
        src = lax.rem(me + d, 16)
        pltpu.make_async_remote_copy(
            src_ref=part.at[0], dst_ref=land.at[src],
            send_sem=asend.at[0], recv_sem=arecv.at[src],
            device_id=here.partner(), device_id_type=MESH,
        ).wait_recv()
        total = total + land[src].astype(F32)
    out_ref[...] = total
    gg.drain()
    mg.drain()
    for c in copies:
        c.wait_send()


VM = pl.BlockSpec(memory_space=pltpu.VMEM)
SM = pl.BlockSpec(memory_space=pltpu.SMEM)
DMA = pltpu.SemaphoreType.DMA


def sds(shape, dtype):
    return jax.ShapeDtypeStruct(shape, dtype)


def params(cid):
    return pltpu.CompilerParams(
        collective_id=cid, has_side_effects=True, vmem_limit_bytes=60 * 1024 * 1024
    )


def per_device(
    tokens, qkv_weight, out_weight, mask_blocks, owner_map, pred_stream, pred_up, pred_down,
    pred_proj,
):
    tok = tokens[0]
    x = lax.axis_index("batch")
    seq = lax.axis_index("seq")
    y = lax.rem(lax.div(seq, 2), 4)
    k = lax.rem(seq, 2)
    pieces = [
        jnp.pad(
            lax.dynamic_slice(qkv_weight, (0, t * D + 352 * y), (352, 352)), ((0, 0), (0, 32))
        )
        for t in range(3)
    ]
    wgrp = jnp.concatenate(pieces, axis=1)
    owners = lax.dynamic_slice(owner_map, (0, 4 * lax.div(seq, 2)), (4, 4)).reshape(4, 2, 2)
    own_here = lax.dynamic_slice(owners, (0, k, 0), (4, 1, 2))[:, 0]
    stream = pred_stream[0].reshape(4, 2, BLK, PD)
    first = (own_here[:, 0] == x)[:, None, None]
    spick = jnp.where(first, stream[:, 0], stream[:, 1]).reshape(4 * BLK, PD)
    owner_tab = jnp.concatenate([owners, lax.dynamic_slice(owners, (x, 0, 0), (1, 2, 2))], axis=0)
    masks = lax.dynamic_slice(mask_blocks, (x, 0), (1, mask_blocks.shape[1]))
    row_block = seq * 2 + lax.broadcasted_iota(jnp.int32, (ROWS, 1), 0) // BLK
    live = jnp.any(masks == row_block, axis=1, keepdims=True).astype(F32)
    live = live / float(4 * mask_blocks.shape[1])

    qkv, kvp, pred, mnorm, rstd, nall, hid, slope, pds = pl.pallas_call(
        qkv_kernel,
        out_shape=(
            sds((4, 512, GRP), BF), sds((4, 512, 256), BF), sds((ROWS, D), F32),
            sds((ROWS, PD), F32), sds((ROWS, 1), F32), sds((1024, PD), BF),
            sds((1024, HS), BF), sds((1024, HS), F32), sds((HS, PD), BF),
        ),
        in_specs=[VM] * 6 + [SM],
        out_specs=(VM,) * 9,
        scratch_shapes=[
            pltpu.VMEM((512, D), BF), pltpu.VMEM((512, D), BF), pltpu.VMEM((D, 3 * GRP), BF),
            pltpu.VMEM((2, 1024, PD), BF), pltpu.VMEM((4, 512, GRP), BF),
            pltpu.VMEM((2, 256, GRP), BF), DMA((40,)), DMA((40,)), DMA((3,)),
        ],
        compiler_params=params(1),
        name="project",
    )(tok, wgrp, spick, pred_up, pred_down, pred_proj, owner_tab)

    att, wout = pl.pallas_call(
        attend_kernel,
        out_shape=(sds((16, 128, 128), BF), sds((D + 32, D), BF)),
        in_specs=[VM] * 3,
        out_specs=(VM, VM),
        scratch_shapes=[
            pltpu.VMEM((16, 128, 128), BF), DMA((9,)), DMA((9,)), DMA((16,)), DMA((16,)),
            DMA((2,)),
        ],
        compiler_params=params(2),
        name="attend",
    )(qkv, kvp, out_weight)

    share = pl.pallas_call(
        grads_kernel,
        out_shape=sds((16, 2 * PD), F32),
        in_specs=[VM] * 12,
        out_specs=VM,
        scratch_shapes=[
            pltpu.VMEM((ROWS, PD), BF), pltpu.VMEM((2, 512, PD), BF),
            pltpu.VMEM((16, 16, 2 * PD), BF), pltpu.VMEM((16, 16, 2 * PD), BF),
            DMA((10,)), DMA((10,)), DMA((16,)), DMA((16,)), DMA((1,)),
        ],
        compiler_params=params(3),
        name="grads",
    )(att, wout, tok, live, pred, mnorm, rstd, nall, hid, slope, pds, pred_proj)
    return share[:12, :PD].T, share[:12, PD:]


def solution(mesh):
    in_specs = (
        P("batch", "seq", None),
        P("batch", None),
        P("batch", None),
        P(),
        P(),
        P("batch", None, "seq", None),
        P(),
        P(),
        P(),
    )
    out_specs = (P(None, ("seq", "batch")), P(("seq", "batch"), None))
    return jax.shard_map(
        per_device, mesh=mesh, in_specs=in_specs, out_specs=out_specs, check_vma=False
    )
```

```python
import functools

import jax
import jax.numpy as jnp
from jax import lax
from jax.experimental import pallas as pl
from jax.experimental.pallas import tpu as pltpu
from jax.sharding import PartitionSpec as P

MESH = pl.DeviceIdType.MESH
BF = jnp.bfloat16
F32 = jnp.float32

D = 1408
H = 16
HD = 88
PD = 384
PH = 1536
BLK = 64
ROWS = 128
GRP = 384
HS = 256
QM = 512
LOG2E = 1.4426950408889634
NT = (((1,), (1,)), ((), ()))
TN = (((0,), (0,)), ((), ()))

gelu_coef = 0.7978845608
gelu_cube = 0.044715


def mm(a, b, dims=(((1,), (0,)), ((), ()))):
    return lax.dot_general(a, b, dims, preferred_element_type=F32)


def layer_norm(values):
    center = values - jnp.mean(values, axis=-1, keepdims=True)
    variance = jnp.mean(center * center, axis=-1, keepdims=True)
    factor = lax.rsqrt(variance + 1e-06)
    return center * factor, factor


def gelu_parts(values):
    inner = gelu_coef * (values + gelu_cube * values * values * values)
    tangent = jnp.tanh(inner)
    value = 0.5 * values * (1.0 + tangent)
    slope = 0.5 * (1.0 + tangent) + 0.5 * values * (1.0 - tangent * tangent) * gelu_coef * (
        1.0 + 3.0 * gelu_cube * values * values
    )
    return value, slope


class Here:
    def __init__(self):
        self.seq = lax.axis_index("seq")
        self.x = lax.axis_index("batch")
        self.k = lax.rem(self.seq, 2)
        self.y = lax.rem(lax.div(self.seq, 2), 4)
        self.z = lax.div(self.seq, 8)

    def at(self, x=None, y=None, z=None, k=None):
        x = self.x if x is None else x
        y = self.y if y is None else y
        z = self.z if z is None else z
        k = self.k if k is None else k
        return {"seq": (z * 4 + y) * 2 + k, "batch": x}

    def step(self, axis, by):
        pos = lax.rem(getattr(self, axis) + by, 4)
        return pos, self.at(**{axis: pos})

    def partner(self):
        return self.at(k=1 - self.k)


class Net:
    def __init__(self, send, recv):
        self.send, self.recv, self.n = send, recv, 0

    def copy(self, src, dst, dev):
        i = self.n
        self.n += 1
        return pltpu.make_async_remote_copy(
            src_ref=src, dst_ref=dst, send_sem=self.send.at[i], recv_sem=self.recv.at[i],
            device_id=dev, device_id_type=MESH,
        )


def greet(devices):
    barrier = pltpu.get_barrier_semaphore()
    for dev in devices:
        pl.semaphore_signal(barrier, inc=1, device_id=dev, device_id_type=MESH)
    pl.semaphore_wait(barrier, len(devices))


class RingGather:
    def __init__(self, net, here, axis, own, buf, stride, base, rows_a, rows):
        self.net, self.buf = net, buf
        self.stride, self.base, self.ra, self.rows = stride, base, rows_a, rows
        self.me = getattr(here, axis)
        self.right_pos, self.right = here.step(axis, 1)
        self.left_pos, self.left = here.step(axis, 3)
        self.far_pos, _ = here.step(axis, 2)
        rb = rows - rows_a
        a, b = pl.ds(0, rows_a), pl.ds(rows_a, rb)
        self.ra_c = net.copy(own.at[a], self.part(self.me, 0), self.right)
        self.lb_c = net.copy(own.at[b], self.part(self.me, 1), self.left)
        self.rb_c = net.copy(own.at[b], self.part(self.me, 1), self.right)
        self.la_c = net.copy(own.at[a], self.part(self.me, 0), self.left)
        self.fa_c = net.copy(self.part(self.left_pos, 0), self.part(self.left_pos, 0), self.right)
        self.fb_c = net.copy(self.part(self.right_pos, 1), self.part(self.right_pos, 1), self.left)

    def offset(self, pos, part):
        off = pos * self.stride + self.base + (self.ra if part == 1 else 0)
        return pl.multiple_of(off, 16)

    def part(self, pos, part):
        n = self.ra if part == 0 else self.rows - self.ra
        return self.buf.at[pl.ds(self.offset(pos, part), n)]

    def whole(self, pos):
        return self.buf.at[pl.ds(self.offset(pos, 0), self.rows)]

    def start(self):
        for c in (self.ra_c, self.lb_c, self.rb_c, self.la_c):
            c.start()

    def forward(self):
        self.ra_c.wait_recv()
        self.fa_c.start()
        self.lb_c.wait_recv()
        self.fb_c.start()

    def near(self):
        self.rb_c.wait_recv()
        self.la_c.wait_recv()

    def far(self):
        self.fa_c.wait_recv()
        self.fb_c.wait_recv()

    def drain(self):
        for c in (self.ra_c, self.lb_c, self.rb_c, self.la_c, self.fa_c, self.fb_c):
            c.wait_send()


class Mirror:
    def __init__(self, net, here, gather, own):
        self.copies = []
        dev = here.partner()
        if own is not None:
            self.copies.append(net.copy(own, gather.whole(gather.me), dev))
        for pos in (gather.left_pos, gather.right_pos, gather.far_pos):
            w = gather.whole(pos)
            self.copies.append(net.copy(w, w, dev))

    def start(self, which):
        for i in which:
            self.copies[i].start()

    def wait_recv(self):
        for c in self.copies:
            c.wait_recv()

    def drain(self):
        for c in self.copies:
            c.wait_send()


def spread(rows, cols):
    i = lax.broadcasted_iota(jnp.int32, (rows, cols), 0)
    j = lax.broadcasted_iota(jnp.int32, (rows, cols), 1)
    lane = j % 128
    return jnp.where((lane < HD) & (i == (j // 128) * HD + lane), 1.0, 0.0).astype(BF)


def gather_spread(rows, cols):
    i = lax.broadcasted_iota(jnp.int32, (rows, cols), 0)
    j = lax.broadcasted_iota(jnp.int32, (rows, cols), 1)
    lane = i % 128
    return jnp.where((lane < HD) & (j == (i // 128) * HD + lane), 1.0, 0.0).astype(BF)


FAN = (0, 1, 3, 2)


def step_kernel(
    tok_ref, wgrp_ref, spick_ref, ow_ref, up_hbm, down_hbm, proj_hbm, live_ref, owner_ref,
    out_ref,
    tokbuf, normed, wbuf, sbuf, outq, qbuf, kbuf, vbuf, bounce, wout, up_ref, down_ref, proj_ref,
    acc, atts, att, pred, mnorm, rstdb, ups_ref, pds_ref, nall, hid, slope, gm, gmall, part, land,
    send, recv, asend, arecv, gsend, grecv, local,
):
    here = Here()
    net = Net(send, recv)
    peers = [here.step("x", s)[1] for s in (1, 3)] + [here.partner()]
    for dz in range(4):
        for dy in range(4):
            if dz or dy:
                peers.append(here.at(z=lax.rem(here.z + dz, 4), y=lax.rem(here.y + dy, 4)))
    greet(peers)

    count = [0]

    def fetch(src, dst):
        c = pltpu.make_async_copy(src, dst, local.at[count[0]])
        count[0] += 1
        c.start()
        return c

    k_half = pl.ds(pl.multiple_of(176 * here.k, 16), 176)
    gt = RingGather(net, here, "y", tok_ref, tokbuf, 128, 0, 64, 128)
    gw = [
        RingGather(
            net, here, "x", wgrp_ref.at[t, k_half], wbuf.at[t], 352, 176 * here.k, 96, 176
        )
        for t in range(3)
    ]
    mw = [Mirror(net, here, g, None) for g in gw]
    gs = RingGather(net, here, "x", spick_ref, sbuf.at[here.k], 256, 0, 128, 256)
    ms = Mirror(net, here, gs, spick_ref)
    go = RingGather(net, here, "x", ow_ref.at[k_half], wout, 352, 176 * here.k, 96, 176)
    mo = Mirror(net, here, go, None)

    gt.start()
    gw[1].start()
    gw[2].start()
    tok_in = fetch(tok_ref, gt.whole(here.y))
    x_rows = pl.ds(pl.multiple_of(352 * here.x, 16), 352)
    own_w = [fetch(wgrp_ref.at[t], wbuf.at[t, x_rows]) for t in range(3)]
    up_in = fetch(up_hbm, up_ref)
    down_in = fetch(down_hbm, down_ref)
    own_s = fetch(spick_ref, gs.whole(here.x))
    own_o = fetch(ow_ref, wout.at[x_rows])
    proj_in = fetch(proj_hbm, proj_ref)
    wout[pl.ds(D, 32), :] = jnp.zeros((32, D), BF)

    def norm_block(slot, pos):
        value = layer_norm(gt.whole(pos)[...].astype(F32))[0].astype(BF)
        normed[slot * 128:(slot + 1) * 128, :] = value

    tok_in.wait()
    norm_block(0, here.y)
    gw[1].forward()
    gw[0].start()
    up_in.wait()
    down_in.wait()
    i = lax.broadcasted_iota(jnp.int32, (PH, HS), 0)
    j = lax.broadcasted_iota(jnp.int32, (PH, HS), 1)
    unit = ((j // 16) * 2 + here.k) * 48 + here.x * 12 + j % 16
    select = jnp.where((j % 16 < 12) & (i == unit), 1.0, 0.0).astype(BF)
    ups_ref[...] = mm(up_ref[...], select).astype(BF)
    pds_ref[...] = mm(select, down_ref[...], TN).astype(BF)

    gt.forward()
    gw[2].forward()
    gw[1].near()
    mw[1].start([0, 1])
    gw[0].forward()
    gs.start()
    ms.start([0])
    gt.near()
    norm_block(1, gt.right_pos)
    norm_block(2, gt.left_pos)
    gw[2].near()
    mw[2].start([0, 1])
    gw[1].far()
    mw[1].start([2])
    gw[0].near()
    mw[0].start([0, 1])
    gw[2].far()
    mw[2].start([2])
    gt.far()
    norm_block(3, gt.far_pos)
    gw[0].far()
    mw[0].start([2])
    for c in own_w:
        c.wait()

    zr, right = here.step("z", 1)
    zl, left = here.step("z", 3)
    zf, _ = here.step("z", 2)
    lo, hi = pl.ds(0, 256), pl.ds(256, 256)
    bufs = (qbuf, kbuf.at[here.k], vbuf.at[here.k])
    pad = spread(GRP, 512)
    lane = lax.broadcasted_iota(jnp.int32, (1, 512), 1) % 128
    ones = jnp.where(lane >= HD, 1.0, 0.0)
    moves = {}
    for t in (1, 2, 0):
        mw[t].wait_recv()
        rows = mm(normed[...], wbuf[t])
        if t == 0:
            rows = rows * (LOG2E / HD**0.5)
        wide = mm(rows.astype(BF), pad)
        if t == 2:
            wide = wide + ones
        wide = wide.astype(BF)
        for h in range(4):
            outq[t, h] = wide[:, h * 128:(h + 1) * 128]
        buf = bufs[t]
        to_r = net.copy(outq.at[t, zr], buf.at[here.z], right)
        to_l = net.copy(outq.at[t, zl], buf.at[here.z], left)
        far_a = net.copy(outq.at[t, zf, lo], bounce.at[t, 0], right)
        far_b = net.copy(outq.at[t, zf, hi], bounce.at[t, 1], left)
        fwd_a = net.copy(bounce.at[t, 0], buf.at[zl, lo], right)
        fwd_b = net.copy(bounce.at[t, 1], buf.at[zr, hi], left)
        to_r.start()
        to_l.start()
        mine = fetch(outq.at[t, here.z], buf.at[here.z])
        mirror = None
        if t:
            mirror = [net.copy(outq.at[t, here.z], buf.at[here.z], here.partner())]
            mirror[0].start()
            for pos in (zl, zr, zf):
                mirror.append(net.copy(buf.at[pos], buf.at[pos], here.partner()))
        moves[t] = (to_r, to_l, far_a, far_b, fwd_a, fwd_b, mine, mirror)
    for t in (1, 2, 0):
        moves[t][2].start()
        moves[t][3].start()
    gs.forward()
    go.start()

    def pair(dq, dk, first):
        zq = lax.rem(here.z + dq, 4)
        zk = lax.rem(here.z + dk, 4)
        for half in range(512 // QM):
            at = slice(half * QM, (half + 1) * QM)
            q = qbuf[zq, at, :]
            total = None
            for c in range(2):
                p = jnp.exp2(mm(q, kbuf[c, zk], NT)).astype(BF)
                term = mm(p, vbuf[c, zk])
                total = term if total is None else total + term
            acc[dq, at, :] = total if first else acc[dq, at, :] + total

    head = here.y * 4 + here.z

    def back(slot):
        zc = lax.rem(here.z + slot // 4, 4)
        yc = lax.rem(here.y + FAN[slot % 4], 4)
        return pltpu.make_async_remote_copy(
            src_ref=atts.at[slot], dst_ref=att.at[head],
            send_sem=asend.at[slot], recv_sem=arecv.at[head],
            device_id=here.at(z=zc, y=yc), device_id_type=MESH,
        )

    def finish(dq):
        value = acc[dq]
        value = (value / value[:, HD:HD + 1]).astype(BF)
        for n in range(4):
            slot = dq * 4 + n
            atts[slot] = value[n * 128:(n + 1) * 128]
            if slot:
                back(slot).start()

    for t in (1, 2, 0):
        moves[t][6].wait()
    moves[1][7][0].wait_recv()
    moves[2][7][0].wait_recv()
    pair(0, 0, True)

    gs.near()
    ms.start([1, 2])
    gs.far()
    ms.start([3])
    own_s.wait()
    proj_in.wait()
    ms.wait_recv()
    stream = jnp.concatenate(
        [sbuf[here.k, pl.ds(owner_ref[4, here.k, b] * 256 + here.x * 64, 64), :] for b in range(2)],
        axis=0,
    ).astype(F32)
    normed_own = layer_norm(stream)[0].astype(BF)
    hidden = gelu_parts(mm(normed_own, up_ref[...]))[0].astype(BF)
    mixed = stream + mm(hidden, down_ref[...])
    mixed_norm, rstd = layer_norm(mixed)
    mnorm[...] = mixed_norm
    rstdb[...] = jnp.broadcast_to(rstd, (ROWS, 128))
    pred[...] = mm(mixed_norm.astype(BF), proj_ref[...])

    for t in (1, 2):
        moves[t][0].wait_recv()
        moves[t][7][1].start()
        moves[t][1].wait_recv()
        moves[t][7][2].start()
    for t in (1, 2, 0):
        moves[t][2].wait_recv()
        moves[t][4].start()
        moves[t][3].wait_recv()
        moves[t][5].start()
    go.forward()
    for t in (1, 2):
        moves[t][7][1].wait_recv()
        moves[t][7][2].wait_recv()
    pair(0, 1, False)
    pair(0, 3, False)
    moves[0][0].wait_recv()
    moves[0][1].wait_recv()
    for dq in (1, 3):
        for dk in (0, 1, 3):
            pair(dq, dk, dk == 0)
    go.near()
    mo.start([0, 1])
    for t in (1, 2):
        moves[t][4].wait_recv()
        moves[t][5].wait_recv()
        moves[t][7][3].start()
    for t in (1, 2):
        moves[t][7][3].wait_recv()
    moves[0][4].wait_recv()
    moves[0][5].wait_recv()
    for dk in (2, 0, 1, 3):
        pair(2, dk, dk == 2)
    finish(2)
    go.far()
    mo.start([2])
    pair(1, 2, False)
    finish(1)
    pair(3, 2, False)
    finish(3)
    pair(0, 2, False)
    finish(0)
    own_a = fetch(atts.at[0], att.at[head])
    own_o.wait()
    mo.wait_recv()
    own_a.wait()
    for d in range(1, 16):
        src = lax.rem(head + d, 16)
        pltpu.make_async_remote_copy(
            src_ref=atts.at[0], dst_ref=att.at[src],
            send_sem=asend.at[0], recv_sem=arecv.at[src],
            device_id=here.partner(), device_id_type=MESH,
        ).wait_recv()

    pack = gather_spread(512, GRP)
    total = gt.whole(here.y)[...].astype(F32)
    for x in range(4):
        wide = jnp.concatenate([att[4 * x + h] for h in range(4)], axis=1)
        total = total + mm(mm(wide, pack).astype(BF), wout[352 * x:352 * x + GRP, :])
    target = layer_norm(total)[0].astype(BF).astype(F32)
    grad_pred = ((pred[...] - target) * live_ref[...]).astype(BF)
    grad_norm = mm(grad_pred, proj_ref[...], NT)
    mixed_norm = mnorm[...]
    first_mean = jnp.mean(grad_norm, axis=-1, keepdims=True)
    second_mean = jnp.mean(grad_norm * mixed_norm, axis=-1, keepdims=True)
    gm[...] = (rstdb[:, 0:1] * (grad_norm - first_mean - mixed_norm * second_mean)).astype(BF)

    gg = RingGather(net, here, "x", gm, gmall.at[here.k], 128, 0, 64, 128)
    mg = Mirror(net, here, gg, gm)
    gg.start()
    mg.start([0])
    own_g = fetch(gm, gg.whole(here.x))

    def share(c):
        for k in range(2):
            at = slice((c * 2 + k) * 128, (c * 2 + k + 1) * 128)
            rows = jnp.concatenate(
                [sbuf[k, pl.ds(owner_ref[c, k, b] * 256 + c * 64, 64), :] for b in range(2)],
                axis=0,
            )
            nv = layer_norm(rows.astype(F32))[0].astype(BF)
            nall[at, :] = nv
            value, deriv = gelu_parts(mm(nv, ups_ref[...]))
            hid[at, :] = value.astype(BF)
            slope[at, :] = deriv

    share(0)
    share(1)
    gg.forward()
    gg.near()
    mg.start([1, 2])
    share(2)
    gg.far()
    mg.start([3])
    share(3)
    own_g.wait()
    mg.wait_recv()

    rows = [gmall[k, c * 128:(c + 1) * 128, :] for c in range(4) for k in range(2)]
    grad_mixed = jnp.concatenate(rows, axis=0)
    grad_down = mm(hid[...], grad_mixed, TN)
    grad_hidden = mm(grad_mixed, pds_ref[...], NT)
    grad_pre = (grad_hidden * slope[...]).astype(BF)
    grad_up = mm(grad_pre, nall[...], TN)
    part[:, :, 0:PD] = grad_up.astype(BF).reshape(16, 16, PD)
    part[:, :, PD:2 * PD] = grad_down.astype(BF).reshape(16, 16, PD)

    me = here.z * 4 + here.y
    copies = []
    for d in range(1, 16):
        to = lax.rem(me + d, 16)
        copies.append(
            pltpu.make_async_remote_copy(
                src_ref=part.at[to], dst_ref=land.at[me],
                send_sem=gsend.at[d], recv_sem=grecv.at[me],
                device_id=here.at(z=lax.div(to, 4), y=lax.rem(to, 4)), device_id_type=MESH,
            )
        )
        copies[-1].start()
    for c in [gt, gs, go, gg, ms, mo, mg] + gw + mw:
        c.drain()
    for t in range(3):
        for c in moves[t][:6] + tuple(moves[t][7] or ()):
            c.wait_send()
    for slot in range(1, 16):
        back(slot).wait_send()
    total = part[me].astype(F32)
    for d in range(1, 16):
        src = lax.rem(me + d, 16)
        pltpu.make_async_remote_copy(
            src_ref=part.at[0], dst_ref=land.at[src],
            send_sem=gsend.at[0], recv_sem=grecv.at[src],
            device_id=here.partner(), device_id_type=MESH,
        ).wait_recv()
        total = total + land[src].astype(F32)
    out_ref[...] = total
    for c in copies:
        c.wait_send()


VM = pl.BlockSpec(memory_space=pltpu.VMEM)
ANY = pl.BlockSpec(memory_space=pl.ANY)
SM = pl.BlockSpec(memory_space=pltpu.SMEM)
DMA = pltpu.SemaphoreType.DMA


def sds(shape, dtype):
    return jax.ShapeDtypeStruct(shape, dtype)


def params(cid):
    return pltpu.CompilerParams(
        collective_id=cid, has_side_effects=True, vmem_limit_bytes=60 * 1024 * 1024
    )


def per_device(
    tokens, qkv_weight, out_weight, mask_blocks, owner_map, pred_stream, pred_up, pred_down,
    pred_proj,
):
    tok = tokens[0]
    x = lax.axis_index("batch")
    seq = lax.axis_index("seq")
    y = lax.rem(lax.div(seq, 2), 4)
    k = lax.rem(seq, 2)
    pieces = [
        jnp.pad(
            lax.dynamic_slice(qkv_weight, (0, t * D + 352 * y), (352, 352)), ((0, 0), (0, 32))
        )
        for t in range(3)
    ]
    wgrp = jnp.stack(pieces, axis=0)
    owners = lax.dynamic_slice(owner_map, (0, 4 * lax.div(seq, 2)), (4, 4)).reshape(4, 2, 2)
    own_here = lax.dynamic_slice(owners, (0, k, 0), (4, 1, 2))[:, 0]
    stream = pred_stream[0].reshape(4, 2, BLK, PD)
    first = (own_here[:, 0] == x)[:, None, None]
    spick = jnp.where(first, stream[:, 0], stream[:, 1]).reshape(4 * BLK, PD)
    owner_tab = jnp.concatenate([owners, lax.dynamic_slice(owners, (x, 0, 0), (1, 2, 2))], axis=0)
    masks = lax.dynamic_slice(mask_blocks, (x, 0), (1, mask_blocks.shape[1]))
    row_block = seq * 2 + lax.broadcasted_iota(jnp.int32, (ROWS, 1), 0) // BLK
    live = jnp.any(masks == row_block, axis=1, keepdims=True).astype(F32)
    live = live / float(4 * mask_blocks.shape[1])

    share = pl.pallas_call(
        step_kernel,
        out_shape=sds((16, 2 * PD), F32),
        in_specs=[ANY] * 7 + [VM, SM],
        out_specs=VM,
        scratch_shapes=[
            pltpu.VMEM((512, D), BF), pltpu.VMEM((512, D), BF), pltpu.VMEM((3, D, GRP), BF),
            pltpu.VMEM((2, 1024, PD), BF), pltpu.VMEM((3, 4, 512, 128), BF),
            pltpu.VMEM((4, 512, 128), BF), pltpu.VMEM((2, 4, 512, 128), BF),
            pltpu.VMEM((2, 4, 512, 128), BF), pltpu.VMEM((3, 2, 256, 128), BF),
            pltpu.VMEM((D + 32, D), BF), pltpu.VMEM((PD, PH), BF), pltpu.VMEM((PH, PD), BF),
            pltpu.VMEM((PD, D), BF), pltpu.VMEM((4, 512, 128), F32),
            pltpu.VMEM((16, 128, 128), BF), pltpu.VMEM((16, 128, 128), BF),
            pltpu.VMEM((ROWS, D), F32), pltpu.VMEM((ROWS, PD), F32), pltpu.VMEM((ROWS, 128), F32),
            pltpu.VMEM((PD, HS), BF), pltpu.VMEM((HS, PD), BF), pltpu.VMEM((1024, PD), BF),
            pltpu.VMEM((1024, HS), BF), pltpu.VMEM((1024, HS), F32), pltpu.VMEM((ROWS, PD), BF),
            pltpu.VMEM((2, 512, PD), BF), pltpu.VMEM((16, 16, 2 * PD), BF),
            pltpu.VMEM((16, 16, 2 * PD), BF),
            DMA((96,)), DMA((96,)), DMA((16,)), DMA((16,)), DMA((16,)), DMA((16,)), DMA((16,)),
        ],
        compiler_params=params(1),
        name="step",
    )(tok, wgrp, spick, out_weight, pred_up, pred_down, pred_proj, live, owner_tab)
    return share[:12, :PD].T, share[:12, PD:]


def solution(mesh):
    in_specs = (
        P("batch", "seq", None),
        P("batch", None),
        P("batch", None),
        P(),
        P(),
        P("batch", None, "seq", None),
        P(),
        P(),
        P(),
    )
    out_specs = (P(None, ("seq", "batch")), P(("seq", "batch"), None))
    return jax.shard_map(
        per_device, mesh=mesh, in_specs=in_specs, out_specs=out_specs, check_vma=False
    )
```

```python
import functools

import jax
import jax.numpy as jnp
from jax import lax
from jax.experimental import pallas as pl
from jax.experimental.pallas import tpu as pltpu
from jax.sharding import PartitionSpec as P

MESH = pl.DeviceIdType.MESH
BF = jnp.bfloat16
F32 = jnp.float32

D = 1408
H = 16
HD = 88
PD = 384
PH = 1536
BLK = 64
ROWS = 128
GRP = 384
HS = 256
QM = 512
LOG2E = 1.4426950408889634
NT = (((1,), (1,)), ((), ()))
TN = (((0,), (0,)), ((), ()))

gelu_coef = 0.7978845608
gelu_cube = 0.044715


def mm(a, b, dims=(((1,), (0,)), ((), ()))):
    return lax.dot_general(a, b, dims, preferred_element_type=F32)


def layer_norm(values):
    center = values - jnp.mean(values, axis=-1, keepdims=True)
    variance = jnp.mean(center * center, axis=-1, keepdims=True)
    factor = lax.rsqrt(variance + 1e-06)
    return center * factor, factor


def gelu_parts(values):
    inner = gelu_coef * (values + gelu_cube * values * values * values)
    tangent = jnp.tanh(inner)
    value = 0.5 * values * (1.0 + tangent)
    slope = 0.5 * (1.0 + tangent) + 0.5 * values * (1.0 - tangent * tangent) * gelu_coef * (
        1.0 + 3.0 * gelu_cube * values * values
    )
    return value, slope


class Here:
    def __init__(self):
        self.seq = lax.axis_index("seq")
        self.x = lax.axis_index("batch")
        self.k = lax.rem(self.seq, 2)
        self.y = lax.rem(lax.div(self.seq, 2), 4)
        self.z = lax.div(self.seq, 8)

    def at(self, x=None, y=None, z=None, k=None):
        x = self.x if x is None else x
        y = self.y if y is None else y
        z = self.z if z is None else z
        k = self.k if k is None else k
        return {"seq": (z * 4 + y) * 2 + k, "batch": x}

    def step(self, axis, by):
        pos = lax.rem(getattr(self, axis) + by, 4)
        return pos, self.at(**{axis: pos})

    def partner(self):
        return self.at(k=1 - self.k)


class Net:
    def __init__(self, send, recv):
        self.send, self.recv, self.n = send, recv, 0

    def copy(self, src, dst, dev):
        i = self.n
        self.n += 1
        return pltpu.make_async_remote_copy(
            src_ref=src, dst_ref=dst, send_sem=self.send.at[i], recv_sem=self.recv.at[i],
            device_id=dev, device_id_type=MESH,
        )


class RingGather:
    def __init__(self, net, here, axis, own, buf, stride, base, rows_a, rows):
        self.net, self.buf = net, buf
        self.stride, self.base, self.ra, self.rows = stride, base, rows_a, rows
        self.me = getattr(here, axis)
        self.right_pos, self.right = here.step(axis, 1)
        self.left_pos, self.left = here.step(axis, 3)
        self.far_pos, _ = here.step(axis, 2)
        rb = rows - rows_a
        a, b = pl.ds(0, rows_a), pl.ds(rows_a, rb)
        self.ra_c = net.copy(own.at[a], self.part(self.me, 0), self.right)
        self.lb_c = net.copy(own.at[b], self.part(self.me, 1), self.left)
        self.rb_c = net.copy(own.at[b], self.part(self.me, 1), self.right)
        self.la_c = net.copy(own.at[a], self.part(self.me, 0), self.left)
        self.fa_c = net.copy(self.part(self.left_pos, 0), self.part(self.left_pos, 0), self.right)
        self.fb_c = net.copy(self.part(self.right_pos, 1), self.part(self.right_pos, 1), self.left)

    def view(self, pos, skip, n):
        if self.stride is None:
            return self.buf.at[pos, pl.ds(pl.multiple_of(self.base + skip, 16), n)]
        return self.buf.at[pl.ds(pl.multiple_of(pos * self.stride + self.base + skip, 16), n)]

    def part(self, pos, part):
        if part == 0:
            return self.view(pos, 0, self.ra)
        return self.view(pos, self.ra, self.rows - self.ra)

    def whole(self, pos):
        return self.view(pos, 0, self.rows)

    def start(self):
        for c in (self.ra_c, self.lb_c, self.rb_c, self.la_c):
            c.start()

    def forward(self):
        self.ra_c.wait_recv()
        self.fa_c.start()
        self.lb_c.wait_recv()
        self.fb_c.start()

    def near(self):
        self.rb_c.wait_recv()
        self.la_c.wait_recv()

    def far(self):
        self.fa_c.wait_recv()
        self.fb_c.wait_recv()

    def drain(self):
        for c in (self.ra_c, self.lb_c, self.rb_c, self.la_c, self.fa_c, self.fb_c):
            c.wait_send()


class Mirror:
    def __init__(self, net, here, gather, own):
        self.copies = []
        dev = here.partner()
        if own is not None:
            self.copies.append(net.copy(own, gather.whole(gather.me), dev))
        for pos in (gather.left_pos, gather.right_pos, gather.far_pos):
            w = gather.whole(pos)
            self.copies.append(net.copy(w, w, dev))

    def start(self, which):
        for i in which:
            self.copies[i].start()

    def wait_recv(self):
        for c in self.copies:
            c.wait_recv()

    def drain(self):
        for c in self.copies:
            c.wait_send()


def spread(rows, cols):
    i = lax.broadcasted_iota(jnp.int32, (rows, cols), 0)
    j = lax.broadcasted_iota(jnp.int32, (rows, cols), 1)
    lane = j % 128
    return jnp.where((lane < HD) & (i == (j // 128) * HD + lane), 1.0, 0.0).astype(BF)


def gather_spread(rows, cols):
    i = lax.broadcasted_iota(jnp.int32, (rows, cols), 0)
    j = lax.broadcasted_iota(jnp.int32, (rows, cols), 1)
    lane = i % 128
    return jnp.where((lane < HD) & (j == (i // 128) * HD + lane), 1.0, 0.0).astype(BF)


FAN = (0, 1, 3, 2)


def step_kernel(
    tok_ref, qkv_hbm, stream_hbm, ow_ref, up_hbm, down_hbm, proj_hbm, mask_hbm, owner_hbm,
    out_ref,
    mask_ref, owner_ref, win, wsend, st, spsend,
    tokbuf, normed, wbuf, sbuf, outq, qpack, kpack, vpack,
    qbuf, kbuf, vbuf, bounce, wout, up_ref, down_ref, proj_ref,
    acc, atts, att, pred, mnorm, rstdb, ups_ref, pds_ref, nall, hid, slope, gm, gmall, part, land,
    send, recv, asend, arecv, gsend, grecv, local,
):
    here = Here()
    net = Net(send, recv)
    peers = [here.step(a, s)[1] for a in ("x", "y", "z") for s in (1, 3)] + [here.partner()]
    barrier = pltpu.get_barrier_semaphore()
    for dev in peers:
        pl.semaphore_signal(barrier, inc=1, device_id=dev, device_id_type=MESH)

    count = [0]

    def fetch(src, dst):
        c = pltpu.make_async_copy(src, dst, local.at[count[0]])
        count[0] += 1
        c.start()
        return c

    first = jnp.minimum(128 * lax.div(11 * here.y, 4), 896)
    skip = 352 * here.y - first
    win_in = {
        t: fetch(qkv_hbm.at[:, pl.ds(pl.multiple_of(t * D + first, 128), 512)], win.at[t])
        for t in (1, 2, 0)
    }
    x_rows = pl.ds(pl.multiple_of(352 * here.x, 16), 352)
    k_half = pl.ds(pl.multiple_of(176 * here.k, 16), 176)
    gt = RingGather(net, here, "y", tok_ref, tokbuf, 128, 0, 64, 128)
    gw = [
        RingGather(net, here, "x", wsend.at[t, k_half], wbuf.at[t], 352, 176 * here.k, 96, 176)
        for t in range(3)
    ]
    mw = [Mirror(net, here, g, None) for g in gw]
    gs = RingGather(net, here, "x", spsend, sbuf.at[here.k], 256, 0, 128, 256)
    ms = Mirror(net, here, gs, spsend)
    part_rows = pl.multiple_of(((here.y % 2) * 2 + here.k) * 96, 96)
    other_rows = pl.multiple_of(((1 - here.y % 2) * 2 + here.k) * 96, 96)
    go = RingGather(
        net, here, "x", wout.at[here.x, pl.ds(part_rows, 96)], wout, None, part_rows, 48, 96
    )
    y_right, y_left = here.step("y", 1)[1], here.step("y", 3)[1]
    given, taken, doubled = [], [], []

    def hand_out(places):
        for pos in places:
            whole = go.whole(pos)
            a, b = go.part(pos, 0), go.part(pos, 1)
            for src, dev in ((whole, here.partner()), (a, y_right), (b, y_left)):
                c = net.copy(src, src, dev)
                c.start()
                given.append(c)

    def hand_in():
        for n, pos in enumerate((go.left_pos, go.right_pos, go.far_pos)):
            given[3 * n + 1].wait_recv()
            given[3 * n + 2].wait_recv()
            whole = wout.at[pos, pl.ds(other_rows, 96)]
            c = net.copy(whole, whole, here.partner())
            c.start()
            taken.append(c)

    tok_in = fetch(tok_ref, gt.whole(here.y))
    owner_in = fetch(owner_hbm, owner_ref)
    mask_in = fetch(mask_hbm, mask_ref)
    st_in = fetch(stream_hbm, st)
    up_in = fetch(up_hbm, up_ref)
    down_in = fetch(down_hbm, down_ref)
    own_o = fetch(ow_ref, wout.at[here.x, pl.ds(0, 352)])
    proj_in = fetch(proj_hbm, proj_ref)
    wout[here.x, pl.ds(352, 32), :] = jnp.zeros((32, D), BF)

    i = lax.broadcasted_iota(jnp.int32, (512, GRP), 0)
    j = lax.broadcasted_iota(jnp.int32, (512, GRP), 1)
    columns = jnp.where((i == j + skip) & (j < 352), 1.0, 0.0).astype(BF)

    def cut(t):
        win_in[t].wait()
        exact = mm(win[t], columns).astype(BF)
        wsend[t] = exact
        wbuf[t, x_rows, :] = exact

    def norm_block(slot, pos):
        value = layer_norm(gt.whole(pos)[...].astype(F32))[0].astype(BF)
        normed[slot * 128:(slot + 1) * 128, :] = value

    group = lax.div(here.seq, 2) * 4

    def owner(c, k, b):
        return owner_ref[c, group + 2 * k + b]

    cut(1)
    pl.semaphore_wait(barrier, len(peers))
    gt.start()
    gw[1].start()
    cut(2)
    gw[2].start()
    cut(0)
    tok_in.wait()
    norm_block(0, here.y)
    gw[1].forward()
    gw[0].start()
    st_in.wait()
    owner_in.wait()
    mask_in.wait()
    for c in range(4):
        block = jnp.where(owner(c, here.k, 0) == here.x, 0, 1)
        rows = st[c, pl.ds(block * 64, 64), :]
        spsend[c * 64:(c + 1) * 64, :] = rows
        sbuf[here.k, pl.ds(pl.multiple_of(here.x * 256 + c * 64, 64), 64), :] = rows
    up_in.wait()
    down_in.wait()
    i = lax.broadcasted_iota(jnp.int32, (PH, HS), 0)
    j = lax.broadcasted_iota(jnp.int32, (PH, HS), 1)
    unit = ((j // 16) * 2 + here.k) * 48 + here.x * 12 + j % 16
    select = jnp.where((j % 16 < 12) & (i == unit), 1.0, 0.0).astype(BF)
    ups_ref[...] = mm(up_ref[...], select).astype(BF)
    pds_ref[...] = mm(select, down_ref[...], TN).astype(BF)

    gt.forward()
    gw[1].near()
    mw[1].start([0, 1])
    gw[2].forward()
    gw[2].near()
    mw[2].start([0, 1])
    gw[1].far()
    mw[1].start([2])
    gw[0].forward()
    own_o.wait()
    go.start()
    gt.near()
    norm_block(1, gt.right_pos)
    norm_block(2, gt.left_pos)
    mw[1].wait_recv()

    zr, right = here.step("z", 1)
    zl, left = here.step("z", 3)
    zf, _ = here.step("z", 2)
    lo, hi = pl.ds(0, 64), pl.ds(64, 64)
    bufs = (qpack, kpack.at[here.k], vpack.at[here.k])
    pad = spread(GRP, 512)
    lane = lax.broadcasted_iota(jnp.int32, (1, 512), 1) % 128
    ones = jnp.where(lane >= HD, 1.0, 0.0)
    slot_of = lax.broadcasted_iota(jnp.int32, (1, GRP), 1) // HD
    near = {t: ([], []) for t in range(3)}
    far, onward, own, mirror = {}, {}, {}, {}
    packed = {}

    def project(t, g0, n):
        rows = mm(normed[g0 * 128:(g0 + n) * 128], wbuf[t])
        if t == 0:
            rows = rows * (LOG2E / HD**0.5)
        for h in range(4):
            value = packed.get((t, h), jnp.zeros((128, GRP), F32))
            for g in range(g0, g0 + n):
                block = rows[(g - g0) * 128:(g - g0 + 1) * 128]
                turn = (HD * (g - h)) % GRP
                if turn:
                    block = pltpu.roll(block, turn, 1)
                value = jnp.where(slot_of == g, block, value)
            if g0 == 0 and n < 4:
                packed[t, h] = value
                outq[t, h, :, 0:256] = value[:, 0:256].astype(BF)
            elif g0 == 0:
                outq[t, h] = value.astype(BF)
            else:
                outq[t, h, :, 256:GRP] = value[:, 256:GRP].astype(BF)
        if g0 == 0:
            at = pl.ds(0, GRP if n == 4 else 256)
        else:
            at = pl.ds(256, 128)
        for pos, dev, into in ((zr, right, near[t][0]), (zl, left, near[t][1])):
            c = net.copy(outq.at[t, pos, :, at], bufs[t].at[here.z, :, at], dev)
            c.start()
            into.append(c)
        if g0 + n == 4:
            buf = bufs[t]
            far[t] = (
                net.copy(outq.at[t, zf, lo], bounce.at[t, 0], right),
                net.copy(outq.at[t, zf, hi], bounce.at[t, 1], left),
            )
            for c in far[t]:
                c.start()
            onward[t] = (
                net.copy(bounce.at[t, 0], buf.at[zl, lo], right),
                net.copy(bounce.at[t, 1], buf.at[zr, hi], left),
            )
            own[t] = fetch(outq.at[t, here.z], buf.at[here.z])
            if t:
                mirror[t] = [net.copy(outq.at[t, here.z], buf.at[here.z], here.partner())]
                mirror[t][0].start()
                for pos in (zl, zr, zf):
                    mirror[t].append(net.copy(buf.at[pos], buf.at[pos], here.partner()))

    def widen(block):
        return mm(block, pad)

    def unpack_q(dz):
        z = lax.rem(here.z + dz, 4)
        wide = widen(qpack[z]).astype(BF)
        for g in range(4):
            qbuf[dz, g * 128:(g + 1) * 128, :] = wide[:, g * 128:(g + 1) * 128]

    def unpack_kv(dz):
        z = lax.rem(here.z + dz, 4)
        for c in range(2):
            for pack_ref, buf, extra in ((kpack, kbuf, None), (vpack, vbuf, ones)):
                wide = widen(pack_ref[c, z])
                if extra is not None:
                    wide = wide + extra
                wide = wide.astype(BF)
                for g in range(4):
                    buf[c, dz, g * 128:(g + 1) * 128, :] = wide[:, g * 128:(g + 1) * 128]

    project(1, 0, 3)
    gw[0].near()
    mw[0].start([0, 1])
    gt.far()
    norm_block(3, gt.far_pos)
    gw[2].far()
    mw[2].start([2])
    project(1, 3, 1)
    mw[2].wait_recv()
    project(2, 0, 4)
    gw[0].far()
    mw[0].start([2])
    mw[0].wait_recv()
    project(0, 0, 4)
    def pair(dq, dk, first):
        for half in range(512 // QM):
            at = slice(half * QM, (half + 1) * QM)
            q = qbuf[dq, at, :]
            total = None
            for c in range(2):
                p = jnp.exp2(mm(q, kbuf[c, dk], NT)).astype(BF)
                term = mm(p, vbuf[c, dk])
                total = term if total is None else total + term
            acc[dq, at, :] = total if first else acc[dq, at, :] + total

    head = here.y * 4 + here.z

    def back(slot):
        zc = lax.rem(here.z + slot // 4, 4)
        yc = lax.rem(here.y + FAN[slot % 4], 4)
        return pltpu.make_async_remote_copy(
            src_ref=atts.at[slot], dst_ref=att.at[head],
            send_sem=asend.at[slot], recv_sem=arecv.at[head],
            device_id=here.at(z=zc, y=yc), device_id_type=MESH,
        )

    def finish(dq):
        value = acc[dq]
        value = (value / value[:, HD:HD + 1]).astype(BF)
        for n in range(4):
            slot = dq * 4 + n
            atts[slot] = value[n * 128:(n + 1) * 128]
            if slot:
                back(slot).start()

    def pass_on(t):
        for a, b in zip(far[t], onward[t]):
            a.wait_recv()
            b.start()

    go.forward()
    gs.start()
    ms.start([0])
    for t in (1, 2, 0):
        own[t].wait()
    mirror[1][0].wait_recv()
    mirror[2][0].wait_recv()
    unpack_q(0)
    unpack_kv(0)
    pair(0, 0, True)
    for t in (1, 2):
        for side in range(2):
            for c in near[t][side]:
                c.wait_recv()
            mirror[t][1 + side].start()
    go.near()
    hand_out([go.left_pos, go.right_pos])
    for t in (1, 2):
        mirror[t][1].wait_recv()
        mirror[t][2].wait_recv()
    unpack_kv(1)
    unpack_kv(3)
    pair(0, 1, False)
    pair(0, 3, False)
    pass_on(1)
    for side in range(2):
        for c in near[0][side]:
            c.wait_recv()
    unpack_q(1)
    unpack_q(3)
    pair(1, 0, True)
    pair(1, 1, False)
    pass_on(2)
    go.far()
    hand_out([go.far_pos])
    pair(1, 3, False)
    pair(3, 0, True)
    pass_on(0)
    gs.forward()
    pair(3, 1, False)
    pair(3, 3, False)
    gs.near()
    ms.start([1, 2])
    for t in (1, 2):
        for c in onward[t]:
            c.wait_recv()
        mirror[t][3].start()
    for t in (1, 2):
        mirror[t][3].wait_recv()
    for c in onward[0]:
        c.wait_recv()
    unpack_q(2)
    unpack_kv(2)
    for dk in (2, 0, 1, 3):
        pair(2, dk, dk == 2)
    finish(2)
    hand_in()
    gs.far()
    ms.start([3])
    pair(1, 2, False)
    finish(1)
    pair(3, 2, False)
    finish(3)
    pair(0, 2, False)
    finish(0)
    own_a = fetch(atts.at[0], att.at[head])

    proj_in.wait()
    ms.wait_recv()
    stream = jnp.concatenate(
        [
            sbuf[here.k, pl.ds(owner(here.x, here.k, b) * 256 + here.x * 64, 64), :]
            for b in range(2)
        ],
        axis=0,
    ).astype(F32)
    normed_own = layer_norm(stream)[0].astype(BF)
    hidden = gelu_parts(mm(normed_own, up_ref[...]))[0].astype(BF)
    mixed = stream + mm(hidden, down_ref[...])
    mixed_norm, rstd = layer_norm(mixed)
    mnorm[...] = mixed_norm
    rstdb[...] = jnp.broadcast_to(rstd, (ROWS, 128))
    pred[...] = mm(mixed_norm.astype(BF), proj_ref[...])

    def share(c):
        for k in range(2):
            at = slice((c * 2 + k) * 128, (c * 2 + k + 1) * 128)
            rows = jnp.concatenate(
                [sbuf[k, pl.ds(owner(c, k, b) * 256 + c * 64, 64), :] for b in range(2)],
                axis=0,
            )
            nv = layer_norm(rows.astype(F32))[0].astype(BF)
            nall[at, :] = nv
            value, deriv = gelu_parts(mm(nv, ups_ref[...]))
            hid[at, :] = value.astype(BF)
            slope[at, :] = deriv

    share(0)
    share(1)
    for n in range(3):
        given[3 * n].wait_recv()
        taken[n].wait_recv()
    own_a.wait()
    for d in range(1, 16):
        src = lax.rem(head + d, 16)
        pltpu.make_async_remote_copy(
            src_ref=atts.at[0], dst_ref=att.at[src],
            send_sem=asend.at[0], recv_sem=arecv.at[src],
            device_id=here.partner(), device_id_type=MESH,
        ).wait_recv()

    pack = gather_spread(512, GRP)
    total = gt.whole(here.y)[...].astype(F32)
    for x in range(4):
        wide = jnp.concatenate([att[4 * x + h] for h in range(4)], axis=1)
        total = total + mm(mm(wide, pack).astype(BF), wout[x])
    target = layer_norm(total)[0].astype(BF).astype(F32)
    masked = mask_ref[pl.ds(here.x, 1), :]
    lives = []
    for b in range(2):
        hit = jnp.where(masked == here.seq * 2 + b, 1.0, 0.0)
        lives.append(jnp.broadcast_to(jnp.max(hit, axis=1, keepdims=True), (BLK, 1)))
    live = jnp.concatenate(lives, axis=0) / float(4 * masked.shape[1])
    grad_pred = ((pred[...] - target) * live).astype(BF)
    grad_norm = mm(grad_pred, proj_ref[...], NT)
    mixed_norm = mnorm[...]
    first_mean = jnp.mean(grad_norm, axis=-1, keepdims=True)
    second_mean = jnp.mean(grad_norm * mixed_norm, axis=-1, keepdims=True)
    grad = (rstdb[:, 0:1] * (grad_norm - first_mean - mixed_norm * second_mean)).astype(BF)
    gm[...] = grad
    gmall[here.k, pl.ds(pl.multiple_of(here.x * 128, 128), 128), :] = grad

    gg = RingGather(net, here, "x", gm, gmall.at[here.k], 128, 0, 64, 128)
    mg = Mirror(net, here, gg, gm)
    gg.start()
    mg.start([0])
    share(2)
    gg.forward()
    share(3)
    gg.near()
    mg.start([1, 2])
    gg.far()
    mg.start([3])
    mg.wait_recv()

    rows = [gmall[k, c * 128:(c + 1) * 128, :] for c in range(4) for k in range(2)]
    grad_mixed = jnp.concatenate(rows, axis=0)
    grad_down = mm(hid[...], grad_mixed, TN)
    grad_hidden = mm(grad_mixed, pds_ref[...], NT)
    grad_pre = (grad_hidden * slope[...]).astype(BF)
    grad_up = mm(grad_pre, nall[...], TN)
    grad_up = grad_up.reshape(16, 2, 8, PD)
    grad_down = grad_down.reshape(16, 2, 8, PD)
    low = lax.broadcasted_iota(jnp.int32, (8, PD), 0) < 4
    part[:, :, 0:PD] = grad_up[:, 0].astype(BF)
    part[:, :, PD:2 * PD] = grad_down[:, 0].astype(BF)
    for d in range(16):
        both = jnp.where(low, grad_up[d, 1], pltpu.roll(grad_down[d, 1], 4, 0))
        part[d, :, 2 * PD:3 * PD] = both.astype(BF)

    me = here.z * 4 + here.y
    copies = []
    for d in range(1, 16):
        to = lax.rem(me + d, 16)
        copies.append(
            pltpu.make_async_remote_copy(
                src_ref=part.at[to], dst_ref=land.at[me],
                send_sem=gsend.at[d], recv_sem=grecv.at[me],
                device_id=here.at(z=lax.div(to, 4), y=lax.rem(to, 4)), device_id_type=MESH,
            )
        )
        copies[-1].start()
    for c in [gt, gs, go, gg, ms, mg] + gw + mw:
        c.drain()
    for c in given + taken:
        c.wait_send()
    for t in range(3):
        for c in near[t][0] + near[t][1] + list(far[t]) + list(onward[t]) + mirror.get(t, []):
            c.wait_send()
    for slot in range(1, 16):
        back(slot).wait_send()
    total = part[me].astype(F32)
    for d in range(1, 16):
        src = lax.rem(me + d, 16)
        pltpu.make_async_remote_copy(
            src_ref=part.at[0], dst_ref=land.at[src],
            send_sem=gsend.at[0], recv_sem=grecv.at[src],
            device_id=here.partner(), device_id_type=MESH,
        ).wait_recv()
        total = total + land[src].astype(F32)
    out_ref[0:8, :] = total[:, 0:2 * PD]
    out_ref[8:12, 0:PD] = total[0:4, 2 * PD:3 * PD]
    out_ref[8:12, PD:2 * PD] = total[4:8, 2 * PD:3 * PD]
    for c in copies:
        c.wait_send()


VM = pl.BlockSpec(memory_space=pltpu.VMEM)
ANY = pl.BlockSpec(memory_space=pl.ANY)
DMA = pltpu.SemaphoreType.DMA


def sds(shape, dtype):
    return jax.ShapeDtypeStruct(shape, dtype)


def params(cid):
    return pltpu.CompilerParams(
        collective_id=cid, has_side_effects=True, vmem_limit_bytes=60 * 1024 * 1024
    )


def per_device(
    tokens, qkv_weight, out_weight, mask_blocks, owner_map, pred_stream, pred_up, pred_down,
    pred_proj,
):
    share = pl.pallas_call(
        step_kernel,
        out_shape=sds((12, 2 * PD), F32),
        in_specs=[ANY] * 9,
        out_specs=VM,
        scratch_shapes=[
            pltpu.VMEM((4, 56), jnp.int32), pltpu.SMEM((4, 64), jnp.int32),
            pltpu.VMEM((3, 352, 512), BF), pltpu.VMEM((3, 352, GRP), BF),
            pltpu.VMEM((4, ROWS, PD), BF), pltpu.VMEM((4 * BLK, PD), BF),
            pltpu.VMEM((512, D), BF), pltpu.VMEM((512, D), BF), pltpu.VMEM((3, D, GRP), BF),
            pltpu.VMEM((2, 1024, PD), BF), pltpu.VMEM((3, 4, 128, GRP), BF),
            pltpu.VMEM((4, 128, GRP), BF), pltpu.VMEM((2, 4, 128, GRP), BF),
            pltpu.VMEM((2, 4, 128, GRP), BF),
            pltpu.VMEM((4, 512, 128), BF), pltpu.VMEM((2, 4, 512, 128), BF),
            pltpu.VMEM((2, 4, 512, 128), BF), pltpu.VMEM((3, 2, 64, GRP), BF),
            pltpu.VMEM((4, GRP, D), BF), pltpu.VMEM((PD, PH), BF), pltpu.VMEM((PH, PD), BF),
            pltpu.VMEM((PD, D), BF), pltpu.VMEM((4, 512, 128), F32),
            pltpu.VMEM((16, 128, 128), BF), pltpu.VMEM((16, 128, 128), BF),
            pltpu.VMEM((ROWS, D), F32), pltpu.VMEM((ROWS, PD), F32), pltpu.VMEM((ROWS, 128), F32),
            pltpu.VMEM((PD, HS), BF), pltpu.VMEM((HS, PD), BF), pltpu.VMEM((1024, PD), BF),
            pltpu.VMEM((1024, HS), BF), pltpu.VMEM((1024, HS), F32), pltpu.VMEM((ROWS, PD), BF),
            pltpu.VMEM((2, 512, PD), BF), pltpu.VMEM((16, 8, 3 * PD), BF),
            pltpu.VMEM((16, 8, 3 * PD), BF),
            DMA((128,)), DMA((128,)), DMA((16,)), DMA((16,)), DMA((16,)), DMA((16,)), DMA((24,)),
        ],
        compiler_params=params(1),
        name="step",
    )(
        tokens[0], qkv_weight, pred_stream[0], out_weight, pred_up, pred_down, pred_proj,
        mask_blocks, owner_map,
    )
    return share[:, :PD].T, share[:, PD:]


def solution(mesh):
    in_specs = (
        P("batch", "seq", None),
        P("batch", None),
        P("batch", None),
        P(),
        P(),
        P("batch", None, "seq", None),
        P(),
        P(),
        P(),
    )
    out_specs = (P(None, ("seq", "batch")), P(("seq", "batch"), None))
    return jax.shard_map(
        per_device, mesh=mesh, in_specs=in_specs, out_specs=out_specs, check_vma=False
    )
```

```python
import functools

import jax
import jax.numpy as jnp
from jax import lax
from jax.experimental import pallas as pl
from jax.experimental.pallas import tpu as pltpu
from jax.sharding import PartitionSpec as P

MESH = pl.DeviceIdType.MESH
BF = jnp.bfloat16
F32 = jnp.float32

D = 1408
H = 16
HD = 88
PD = 384
PH = 1536
BLK = 64
ROWS = 128
GRP = 384
HS = 256
QM = 512
LOG2E = 1.4426950408889634
NT = (((1,), (1,)), ((), ()))
TN = (((0,), (0,)), ((), ()))

gelu_coef = 0.7978845608
gelu_cube = 0.044715


def mm(a, b, dims=(((1,), (0,)), ((), ()))):
    return lax.dot_general(a, b, dims, preferred_element_type=F32)


def layer_norm(values):
    center = values - jnp.mean(values, axis=-1, keepdims=True)
    variance = jnp.mean(center * center, axis=-1, keepdims=True)
    factor = lax.rsqrt(variance + 1e-06)
    return center * factor, factor


def gelu_parts(values):
    inner = gelu_coef * (values + gelu_cube * values * values * values)
    tangent = jnp.tanh(inner)
    value = 0.5 * values * (1.0 + tangent)
    slope = 0.5 * (1.0 + tangent) + 0.5 * values * (1.0 - tangent * tangent) * gelu_coef * (
        1.0 + 3.0 * gelu_cube * values * values
    )
    return value, slope


class Here:
    def __init__(self):
        self.seq = lax.axis_index("seq")
        self.x = lax.axis_index("batch")
        self.k = lax.rem(self.seq, 2)
        self.y = lax.rem(lax.div(self.seq, 2), 4)
        self.z = lax.div(self.seq, 8)

    def at(self, x=None, y=None, z=None, k=None):
        x = self.x if x is None else x
        y = self.y if y is None else y
        z = self.z if z is None else z
        k = self.k if k is None else k
        return {"seq": (z * 4 + y) * 2 + k, "batch": x}

    def step(self, axis, by):
        pos = lax.rem(getattr(self, axis) + by, 4)
        return pos, self.at(**{axis: pos})

    def partner(self):
        return self.at(k=1 - self.k)


class Net:
    def __init__(self, here, send, recv):
        self.dev, self.send, self.recv = here.partner(), send, recv
        self.sends = self.recvs = 0

    def out(self):
        self.sends += 1
        return self.send.at[self.sends - 1]

    def into(self):
        self.recvs += 1
        return self.recv.at[self.recvs - 1]

    def copy(self, src, dst, dev, send_sem, recv_sem):
        return pltpu.make_async_remote_copy(
            src_ref=src, dst_ref=dst, send_sem=send_sem, recv_sem=recv_sem,
            device_id=dev, device_id_type=MESH,
        )

    def sent(self, sem, view):
        self.copy(view, view, self.dev, sem, sem).wait_send()

    def came(self, sem, view):
        self.copy(view, view, self.dev, sem, sem).wait_recv()


class RingGather:
    def __init__(self, net, here, axis, own, view, rows_a, rows, three):
        self.net, self.view, self.ra, self.rows, self.three = net, view, rows_a, rows, three
        self.me = getattr(here, axis)
        self.right_pos, self.right = here.step(axis, 1)
        self.left_pos, self.left = here.step(axis, 3)
        self.far_pos, _ = here.step(axis, 2)
        a, b = pl.ds(0, rows_a), pl.ds(rows_a, rows - rows_a)
        self.left_in, self.right_in, self.near_in, self.far_in = (net.into() for _ in range(4))
        self.done_out = s = net.out()
        mine_a, mine_b = self.part(self.me, 0), self.part(self.me, 1)
        self.copies = (
            net.copy(own.at[a], mine_a, self.right, s, self.left_in),
            net.copy(own.at[b], mine_b, self.left, s, self.right_in),
            net.copy(own.at[b], mine_b, self.right, s, self.near_in),
            net.copy(own.at[a], mine_a, self.left, s, self.near_in),
        )
        from_left, from_right = self.part(self.left_pos, 0), self.part(self.right_pos, 1)
        self.on = (
            net.copy(from_left, from_left, self.right, s, self.far_in),
            net.copy(from_right, from_right, self.left, s, self.far_in),
        )

    def part(self, pos, part):
        if part == 0:
            return self.view(pos, 0, self.ra)
        return self.view(pos, self.ra, self.rows - self.ra)

    def whole(self, pos):
        return self.view(pos, 0, self.rows)

    def start(self):
        for c in self.copies:
            c.start()

    def forward(self):
        self.net.came(self.left_in, self.part(self.left_pos, 0))
        self.on[0].start()
        self.net.came(self.right_in, self.part(self.right_pos, 1))
        self.on[1].start()

    def near(self):
        self.net.came(self.near_in, self.whole(self.me))

    def far(self):
        self.net.came(self.far_in, self.whole(self.me))

    def drain(self):
        self.net.sent(self.done_out, self.three)


class Mirror:
    def __init__(self, net, here, gather, own, total, groups):
        self.net, self.total = net, total
        self.done_out = net.out()
        self.ins = [(net.into(), view) for _, view in groups]
        sem_of = {n: self.ins[i][0] for i, (ns, _) in enumerate(groups) for n in ns}
        blocks = [] if own is None else [(own, gather.whole(gather.me))]
        for pos in (gather.left_pos, gather.right_pos, gather.far_pos):
            blocks.append((gather.whole(pos), gather.whole(pos)))
        self.copies = [
            net.copy(src, dst, here.partner(), self.done_out, sem_of[n])
            for n, (src, dst) in enumerate(blocks)
        ]

    def start(self, which):
        for i in which:
            self.copies[i].start()

    def wait_recv(self, group=0):
        self.net.came(*self.ins[group])

    def drain(self):
        self.net.sent(self.done_out, self.total)


class Halves:
    def __init__(self, net, here, gather, other, axis, three, six, nine):
        self.net, self.gather, self.other = net, gather, other
        self.three, self.six, self.nine = three, six, nine
        self.right, self.left = here.step(axis, 1)[1], here.step(axis, 3)[1]
        self.partner = here.partner()
        self.done_out, self.half_in, self.done_in = net.out(), net.into(), net.into()

    def pass_on(self, src, dev, sem):
        self.net.copy(src, src, dev, self.done_out, sem).start()

    def hand_out(self, places):
        g = self.gather
        for pos in places:
            self.pass_on(g.whole(pos), self.partner, self.done_in)
            self.pass_on(g.part(pos, 0), self.right, self.half_in)
            self.pass_on(g.part(pos, 1), self.left, self.half_in)

    def near(self):
        self.gather.near()
        self.hand_out([self.gather.left_pos, self.gather.right_pos])

    def far(self):
        self.gather.far()
        self.hand_out([self.gather.far_pos])

    def hand_in(self):
        g = self.gather
        self.net.came(self.half_in, self.three)
        for pos in (g.left_pos, g.right_pos, g.far_pos):
            self.pass_on(self.other(pos), self.partner, self.done_in)

    def done(self):
        self.net.came(self.done_in, self.six)

    def drain(self):
        self.gather.drain()
        self.net.sent(self.done_out, self.nine)


def spread(rows, cols):
    i = lax.broadcasted_iota(jnp.int32, (rows, cols), 0)
    j = lax.broadcasted_iota(jnp.int32, (rows, cols), 1)
    lane = j % 128
    return jnp.where((lane < HD) & (i == (j // 128) * HD + lane), 1.0, 0.0).astype(BF)


def gather_spread(rows, cols):
    i = lax.broadcasted_iota(jnp.int32, (rows, cols), 0)
    j = lax.broadcasted_iota(jnp.int32, (rows, cols), 1)
    lane = i % 128
    return jnp.where((lane < HD) & (j == (i // 128) * HD + lane), 1.0, 0.0).astype(BF)


FAN = (0, 1, 3, 2)


def step_kernel(
    tok_ref, qkv_hbm, stream_hbm, ow_ref, up_hbm, down_hbm, proj_hbm, mask_hbm, owner_hbm,
    out_ref,
    mask_ref, owner_ref, win, wsend, st, spsend,
    tokbuf, normed, wbuf, sbuf, outq, qpack, kpack, vpack,
    qbuf, kbuf, vbuf, wout, up_ref, down_ref, proj_ref,
    acc, atts, att, pred, mnorm, rstdb, ups_ref, pds_ref, nall, hid, slope, gm, gmall, part, land,
    send, recv, asend, arecv, gsend, grecv, local,
):
    here = Here()
    net = Net(here, send, recv)
    peers = [here.step(a, s)[1] for a in ("x", "y", "z") for s in (1, 3)] + [here.partner(), here.step("z", 2)[1]]
    barrier = pltpu.get_barrier_semaphore()
    for dev in peers:
        pl.semaphore_signal(barrier, inc=1, device_id=dev, device_id_type=MESH)

    count = [0]

    def fetch(src, dst):
        c = pltpu.make_async_copy(src, dst, local.at[count[0]])
        count[0] += 1
        c.start()
        return c

    first = jnp.minimum(128 * lax.div(11 * here.y, 4), 896)
    skip = 352 * here.y - first
    win_in = {
        t: fetch(qkv_hbm.at[:, pl.ds(pl.multiple_of(t * D + first, 128), 512)], win.at[t])
        for t in (1, 2, 0)
    }
    def rows_at(ref, stride, base=0):
        return lambda pos, skip, n: ref.at[pl.ds(pl.multiple_of(pos * stride + base + skip, 16), n)]

    gt = RingGather(
        net, here, "y", tok_ref, rows_at(tokbuf, 128), 64, 128,
        tokbuf.at[pl.ds(0, 384)],
    )
    k_half = pl.ds(pl.multiple_of(176 * here.k, 16), 176)
    gw = [
        RingGather(
            net, here, "x", wsend.at[t, k_half], rows_at(wbuf.at[t], 352, 176 * here.k), 96, 176,
            wbuf.at[t, pl.ds(0, 528)],
        )
        for t in range(3)
    ]
    mw = [Mirror(net, here, g, None, g.three, [((0, 1, 2), g.three)]) for g in gw]
    gs = RingGather(
        net, here, "x", spsend, rows_at(sbuf.at[here.k], 256), 128, 256, sbuf.at[0, pl.ds(0, 768)]
    )
    ms = Mirror(net, here, gs, spsend, sbuf.at[0], [((0, 1, 2, 3), sbuf.at[0])])
    part_rows = pl.multiple_of(((here.y % 2) * 2 + here.k) * 96, 96)
    other_rows = pl.multiple_of(((1 - here.y % 2) * 2 + here.k) * 96, 96)
    go = RingGather(
        net, here, "x", wout.at[here.x, pl.ds(part_rows, 96)],
        lambda pos, skip, n: wout.at[pos, pl.ds(pl.multiple_of(part_rows + skip, 16), n)], 48, 96,
        wout.at[pl.ds(0, 3), pl.ds(0, 96)],
    )
    ho = Halves(
        net, here, go, lambda pos: wout.at[pos, pl.ds(other_rows, 96)], "y",
        *[wout.at[pl.ds(0, 3), pl.ds(0, 96 * n)] for n in (1, 2, 3)],
    )
    tok_in = fetch(tok_ref, gt.whole(here.y))
    owner_in = fetch(owner_hbm, owner_ref)
    mask_in = fetch(mask_hbm, mask_ref)
    st_in = fetch(stream_hbm, st)
    up_in = fetch(up_hbm, up_ref)
    down_in = fetch(down_hbm, down_ref)
    own_o = fetch(ow_ref, wout.at[here.x, pl.ds(0, 352)])
    proj_in = fetch(proj_hbm, proj_ref)
    wout[here.x, pl.ds(352, 32), :] = jnp.zeros((32, D), BF)

    i = lax.broadcasted_iota(jnp.int32, (512, GRP), 0)
    j = lax.broadcasted_iota(jnp.int32, (512, GRP), 1)
    columns = jnp.where((i == j + skip) & (j < 352), 1.0, 0.0).astype(BF)

    def cut(t):
        win_in[t].wait()
        exact = mm(win[t], columns).astype(BF)
        wsend[t] = exact
        wbuf[t, pl.ds(pl.multiple_of(352 * here.x, 16), 352), :] = exact

    def norm_block(slot, pos):
        value = layer_norm(gt.whole(pos)[...].astype(F32))[0].astype(BF)
        normed[slot * 128:(slot + 1) * 128, :] = value

    first_block = lax.div(here.seq, 2) * 4

    def owner(c, k, b):
        return owner_ref[c, first_block + 2 * k + b]

    cut(1)
    pl.semaphore_wait(barrier, len(peers))
    gt.start()
    gw[1].start()
    cut(2)
    gw[2].start()
    cut(0)
    tok_in.wait()
    norm_block(0, here.y)
    gw[1].forward()
    gw[0].start()
    st_in.wait()
    owner_in.wait()
    mask_in.wait()
    for c in range(4):
        block = jnp.where(owner(c, here.k, 0) == here.x, 0, 1)
        rows = st[c, pl.ds(block * 64, 64), :]
        spsend[c * 64:(c + 1) * 64, :] = rows
        sbuf[here.k, pl.ds(pl.multiple_of(here.x * 256 + c * 64, 64), 64), :] = rows
    up_in.wait()
    down_in.wait()
    i = lax.broadcasted_iota(jnp.int32, (PH, HS), 0)
    j = lax.broadcasted_iota(jnp.int32, (PH, HS), 1)
    unit = ((j // 16) * 2 + here.k) * 48 + here.x * 12 + j % 16
    select = jnp.where((j % 16 < 12) & (i == unit), 1.0, 0.0).astype(BF)
    ups_ref[...] = mm(up_ref[...], select).astype(BF)
    pds_ref[...] = mm(select, down_ref[...], TN).astype(BF)

    gt.forward()
    gw[1].near()
    mw[1].start([0, 1])
    gw[2].forward()
    gw[2].near()
    mw[2].start([0, 1])
    gw[1].far()
    mw[1].start([2])
    gw[0].forward()
    own_o.wait()
    go.start()
    gt.near()
    norm_block(1, gt.right_pos)
    norm_block(2, gt.left_pos)
    mw[1].wait_recv()

    zr, right = here.step("z", 1)
    zl, left = here.step("z", 3)
    zf, across = here.step("z", 2)
    bufs = (qpack, kpack.at[here.k], vpack.at[here.k])
    pad = spread(GRP, 512)
    lane = lax.broadcasted_iota(jnp.int32, (1, 512), 1) % 128
    ones = jnp.where(lane >= HD, 1.0, 0.0)
    slot_of = lax.broadcasted_iota(jnp.int32, (1, GRP), 1) // HD
    head_out = [net.out() for _ in range(3)]
    near_in = [net.into() for _ in range(3)]
    far_in = [net.into(), net.into()]
    pass_out = net.out()
    pass_in = [net.into() for _ in range(3)]
    own = {}

    def pass_head(t, src, pos, group):
        buf = bufs[t]
        src = buf.at[pos] if src is None else src
        net.copy(src, buf.at[pos], here.partner(), pass_out, pass_in[group]).start()

    packed = {}

    def project(t, g0, n):
        rows = mm(normed[g0 * 128:(g0 + n) * 128], wbuf[t])
        if t == 0:
            rows = rows * (LOG2E / HD**0.5)
        for h in range(4):
            value = packed.get((t, h), jnp.zeros((128, GRP), F32))
            for g in range(g0, g0 + n):
                block = rows[(g - g0) * 128:(g - g0 + 1) * 128]
                turn = (HD * (g - h)) % GRP
                if turn:
                    block = pltpu.roll(block, turn, 1)
                value = jnp.where(slot_of == g, block, value)
            if g0 == 0 and n < 4:
                packed[t, h] = value
                outq[t, h, :, 0:256] = value[:, 0:256].astype(BF)
            elif g0 == 0:
                outq[t, h] = value.astype(BF)
            else:
                outq[t, h, :, 256:GRP] = value[:, 256:GRP].astype(BF)
        if g0 == 0:
            at = pl.ds(0, GRP if n == 4 else 256)
        else:
            at = pl.ds(256, 128)
        for pos, dev in ((zr, right), (zl, left)):
            net.copy(
                outq.at[t, pos, :, at], bufs[t].at[here.z, :, at], dev, head_out[t], near_in[t]
            ).start()
        if g0 + n == 4:
            net.copy(
                outq.at[t, zf], bufs[t].at[here.z], across, head_out[t], far_in[1 if t else 0]
            ).start()
            own[t] = fetch(outq.at[t, here.z], bufs[t].at[here.z])
            if t:
                pass_head(t, outq.at[t, here.z], here.z, 0)

    def widen(block):
        return mm(block, pad)

    def unpack_q(dz):
        z = lax.rem(here.z + dz, 4)
        wide = widen(qpack[z]).astype(BF)
        for g in range(4):
            qbuf[dz, g * 128:(g + 1) * 128, :] = wide[:, g * 128:(g + 1) * 128]

    def unpack_kv(dz, cores=(0, 1)):
        z = lax.rem(here.z + dz, 4)
        for c in cores:
            core = 1 - here.k if c else here.k
            for pack_ref, buf, extra in ((kpack, kbuf, None), (vpack, vbuf, ones)):
                wide = widen(pack_ref[core, z])
                if extra is not None:
                    wide = wide + extra
                wide = wide.astype(BF)
                for g in range(4):
                    buf[c, dz, g * 128:(g + 1) * 128, :] = wide[:, g * 128:(g + 1) * 128]

    project(1, 0, 3)
    gw[0].near()
    mw[0].start([0, 1])
    gt.far()
    norm_block(3, gt.far_pos)
    gw[2].far()
    mw[2].start([2])
    project(1, 3, 1)
    mw[2].wait_recv()
    project(2, 0, 4)
    gw[0].far()
    mw[0].start([2])
    mw[0].wait_recv()
    project(0, 0, 4)

    def pair(dq, dk, first, cores=(0, 1)):
        for half in range(512 // QM):
            at = slice(half * QM, (half + 1) * QM)
            q = qbuf[dq, at, :]
            total = None
            for c in cores:
                p = jnp.exp2(mm(q, kbuf[c, dk], NT)).astype(BF)
                term = mm(p, vbuf[c, dk])
                total = term if total is None else total + term
            acc[dq, at, :] = total if first else acc[dq, at, :] + total

    head = here.y * 4 + here.z

    def back(slot):
        zc = lax.rem(here.z + slot // 4, 4)
        yc = lax.rem(here.y + FAN[slot % 4], 4)
        return pltpu.make_async_remote_copy(
            src_ref=atts.at[slot], dst_ref=att.at[head],
            send_sem=asend.at[0], recv_sem=arecv.at[here.y],
            device_id=here.at(z=zc, y=yc), device_id_type=MESH,
        )

    def finish(dq):
        value = acc[dq]
        value = (value / value[:, HD:HD + 1]).astype(BF)
        for n in range(4):
            slot = dq * 4 + n
            atts[slot] = value[n * 128:(n + 1) * 128]
            if slot:
                back(slot).start()

    go.forward()
    gs.start()
    ms.start([0])
    for t in (1, 2, 0):
        own[t].wait()
    unpack_q(0)
    unpack_kv(0, (0,))
    pair(0, 0, True, (0,))
    net.came(pass_in[0], kpack.at[0, pl.ds(0, 2)])
    unpack_kv(0, (1,))
    pair(0, 0, False, (1,))
    for t in (1, 2):
        net.came(near_in[t], kpack.at[0, pl.ds(0, 2)])
        pass_head(t, None, zl, 1)
        pass_head(t, None, zr, 1)
    ho.near()
    for dk in (1, 3):
        unpack_kv(dk, (0,))
        pair(0, dk, False, (0,))
    net.came(far_in[1], kpack.at[0, pl.ds(0, 2)])
    for t in (1, 2):
        pass_head(t, None, zf, 2)
    net.came(pass_in[1], kpack.at[0])
    for dk in (1, 3):
        unpack_kv(dk, (1,))
        pair(0, dk, False, (1,))
    ho.far()
    gs.forward()
    net.came(near_in[0], kpack.at[0, pl.ds(0, 2)])
    unpack_q(1)
    unpack_q(3)
    for dk in (0, 1, 3):
        pair(1, dk, dk == 0)
    net.came(pass_in[2], kpack.at[0, pl.ds(0, 2)])
    unpack_kv(2)
    pair(1, 2, False)
    finish(1)
    net.came(far_in[0], kpack.at[0, 0])
    gs.near()
    ms.start([1, 2])
    unpack_q(2)
    for dk in (2, 0, 1, 3):
        pair(2, dk, dk == 2)
    finish(2)
    gs.far()
    ms.start([3])
    for dk in (0, 1, 2, 3):
        pair(3, dk, dk == 0)
    finish(3)
    ho.hand_in()
    pair(0, 2, False)
    finish(0)
    own_a = fetch(atts.at[0], att.at[head])

    proj_in.wait()
    ms.wait_recv()
    stream = jnp.concatenate(
        [
            sbuf[here.k, pl.ds(owner(here.x, here.k, b) * 256 + here.x * 64, 64), :]
            for b in range(2)
        ],
        axis=0,
    ).astype(F32)
    normed_own = layer_norm(stream)[0].astype(BF)
    hidden = gelu_parts(mm(normed_own, up_ref[...]))[0].astype(BF)
    mixed = stream + mm(hidden, down_ref[...])
    mixed_norm, rstd = layer_norm(mixed)
    mnorm[...] = mixed_norm
    rstdb[...] = jnp.broadcast_to(rstd, (ROWS, 128))
    pred[...] = mm(mixed_norm.astype(BF), proj_ref[...])

    def share(slot):
        c = lax.rem(here.x + FAN[slot], 4)
        for k in range(2):
            at = slice((slot * 2 + k) * 128, (slot * 2 + k + 1) * 128)
            rows = jnp.concatenate(
                [sbuf[k, pl.ds(owner(c, k, b) * 256 + c * 64, 64), :] for b in range(2)],
                axis=0,
            )
            nv = layer_norm(rows.astype(F32))[0].astype(BF)
            nall[at, :] = nv
            value, deriv = gelu_parts(mm(nv, ups_ref[...]))
            hid[at, :] = value.astype(BF)
            slope[at, :] = deriv

    share(0)
    share(1)
    ho.done()
    own_a.wait()
    pack = gather_spread(512, GRP)
    total = gt.whole(here.y)[...].astype(F32)
    for dy in (0, 1, 3, 2):
        group = lax.rem(here.y + dy, 4)
        net.came(arecv.at[group], att.at[pl.ds(0, 4 if dy else 3)])
        wide = jnp.concatenate([att[group * 4 + h] for h in range(4)], axis=1)
        total = total + mm(mm(wide, pack).astype(BF), wout[group])
    target = layer_norm(total)[0].astype(BF).astype(F32)
    masked = mask_ref[pl.ds(here.x, 1), :]
    lives = []
    for b in range(2):
        hit = jnp.where(masked == here.seq * 2 + b, 1.0, 0.0)
        lives.append(jnp.broadcast_to(jnp.max(hit, axis=1, keepdims=True), (BLK, 1)))
    live = jnp.concatenate(lives, axis=0) / float(4 * masked.shape[1])
    grad_pred = ((pred[...] - target) * live).astype(BF)
    grad_norm = mm(grad_pred, proj_ref[...], NT)
    mixed_norm = mnorm[...]
    first_mean = jnp.mean(grad_norm, axis=-1, keepdims=True)
    second_mean = jnp.mean(grad_norm * mixed_norm, axis=-1, keepdims=True)
    grad = (rstdb[:, 0:1] * (grad_norm - first_mean - mixed_norm * second_mean)).astype(BF)
    gm[...] = grad
    gmall[here.k, pl.ds(pl.multiple_of(here.x * 128, 128), 128), :] = grad

    gg = RingGather(net, here, "x", gm, rows_at(gmall.at[here.k], 128), 64, 128, gmall.at[0, pl.ds(0, 384)])
    mg = Mirror(
        net, here, gg, gm, gmall.at[0],
        [((0, 1, 2), gmall.at[0, pl.ds(0, 384)]), ((3,), gmall.at[0, pl.ds(0, 128)])],
    )
    gg.start()
    mg.start([0])
    share(2)
    gg.forward()
    share(3)
    gg.near()
    mg.start([1, 2])
    mg.wait_recv(0)

    def grads(slots):
        places = [(gg.me, gg.right_pos, gg.left_pos, gg.far_pos)[n] for n in slots]
        rows = [
            gmall[k, pl.ds(pl.multiple_of(pos * 128, 128), 128), :]
            for pos in places for k in range(2)
        ]
        grad_mixed = jnp.concatenate(rows, axis=0)
        at = slice(slots[0] * 256, (slots[-1] + 1) * 256)
        down = mm(hid[at, :], grad_mixed, TN)
        grad_hidden = mm(grad_mixed, pds_ref[...], NT)
        grad_pre = (grad_hidden * slope[at, :]).astype(BF)
        return mm(grad_pre, nall[at, :], TN), down

    up_near, down_near = grads((0, 1, 2))
    gg.far()
    mg.start([3])
    mg.wait_recv(1)
    grad_up, grad_down = grads((3,))
    grad_up = grad_up + up_near
    grad_down = grad_down + down_near
    grad_up = grad_up.reshape(16, 2, 8, PD)
    grad_down = grad_down.reshape(16, 2, 8, PD)
    low = lax.broadcasted_iota(jnp.int32, (8, PD), 0) < 4
    part[:, :, 0:PD] = grad_up[:, 0].astype(BF)
    part[:, :, PD:2 * PD] = grad_down[:, 0].astype(BF)
    for d in range(16):
        both = jnp.where(low, grad_up[d, 1], pltpu.roll(grad_down[d, 1], 4, 0))
        part[d, :, 2 * PD:3 * PD] = both.astype(BF)

    me = here.z * 4 + here.y
    for d in range(1, 16):
        to = lax.rem(me + d, 16)
        net.copy(
            part.at[to], land.at[me], here.at(z=lax.div(to, 4), y=lax.rem(to, 4)),
            gsend.at[0], grecv.at[0],
        ).start()
    for c in [gt, gs, ho, gg, ms, mg] + gw + mw:
        c.drain()
    for t in range(3):
        net.sent(head_out[t], outq.at[t, pl.ds(0, 3)])
    net.sent(pass_out, kpack)
    net.sent(asend.at[0], atts.at[pl.ds(0, 15)])
    total = part[me].astype(F32)
    net.came(grecv.at[0], land.at[pl.ds(0, 15)])
    for d in range(1, 16):
        total = total + land[lax.rem(me + d, 16)].astype(F32)
    out_ref[0:8, :] = total[:, 0:2 * PD]
    out_ref[8:12, 0:PD] = total[0:4, 2 * PD:3 * PD]
    out_ref[8:12, PD:2 * PD] = total[4:8, 2 * PD:3 * PD]
    net.sent(gsend.at[0], part.at[pl.ds(0, 15)])


VM = pl.BlockSpec(memory_space=pltpu.VMEM)
ANY = pl.BlockSpec(memory_space=pl.ANY)
DMA = pltpu.SemaphoreType.DMA


def sds(shape, dtype):
    return jax.ShapeDtypeStruct(shape, dtype)


def params(cid):
    return pltpu.CompilerParams(
        collective_id=cid, has_side_effects=True, vmem_limit_bytes=60 * 1024 * 1024
    )


def per_device(
    tokens, qkv_weight, out_weight, mask_blocks, owner_map, pred_stream, pred_up, pred_down,
    pred_proj,
):
    share = pl.pallas_call(
        step_kernel,
        out_shape=sds((12, 2 * PD), F32),
        in_specs=[ANY] * 9,
        out_specs=VM,
        scratch_shapes=[
            pltpu.VMEM((4, 56), jnp.int32), pltpu.SMEM((4, 64), jnp.int32),
            pltpu.VMEM((3, 352, 512), BF), pltpu.VMEM((3, 352, GRP), BF),
            pltpu.VMEM((4, ROWS, PD), BF), pltpu.VMEM((4 * BLK, PD), BF),
            pltpu.VMEM((512, D), BF), pltpu.VMEM((512, D), BF), pltpu.VMEM((3, D, GRP), BF),
            pltpu.VMEM((2, 1024, PD), BF), pltpu.VMEM((3, 4, 128, GRP), BF),
            pltpu.VMEM((4, 128, GRP), BF), pltpu.VMEM((2, 4, 128, GRP), BF),
            pltpu.VMEM((2, 4, 128, GRP), BF),
            pltpu.VMEM((4, 512, 128), BF), pltpu.VMEM((2, 4, 512, 128), BF),
            pltpu.VMEM((2, 4, 512, 128), BF),
            pltpu.VMEM((4, GRP, D), BF), pltpu.VMEM((PD, PH), BF), pltpu.VMEM((PH, PD), BF),
            pltpu.VMEM((PD, D), BF), pltpu.VMEM((4, 512, 128), F32),
            pltpu.VMEM((16, 128, 128), BF), pltpu.VMEM((16, 128, 128), BF),
            pltpu.VMEM((ROWS, D), F32), pltpu.VMEM((ROWS, PD), F32), pltpu.VMEM((ROWS, 128), F32),
            pltpu.VMEM((PD, HS), BF), pltpu.VMEM((HS, PD), BF), pltpu.VMEM((1024, PD), BF),
            pltpu.VMEM((1024, HS), BF), pltpu.VMEM((1024, HS), F32), pltpu.VMEM((ROWS, PD), BF),
            pltpu.VMEM((2, 512, PD), BF), pltpu.VMEM((16, 8, 3 * PD), BF),
            pltpu.VMEM((16, 8, 3 * PD), BF),
            DMA((17,)), DMA((44,)), DMA((1,)), DMA((4,)), DMA((1,)), DMA((1,)), DMA((15,)),
        ],
        compiler_params=params(1),
        name="step",
    )(
        tokens[0], qkv_weight, pred_stream[0], out_weight, pred_up, pred_down, pred_proj,
        mask_blocks, owner_map,
    )
    return share[:, :PD].T, share[:, PD:]


def solution(mesh):
    in_specs = (
        P("batch", "seq", None),
        P("batch", None),
        P("batch", None),
        P(),
        P(),
        P("batch", None, "seq", None),
        P(),
        P(),
        P(),
    )
    out_specs = (P(None, ("seq", "batch")), P(("seq", "batch"), None))
    return jax.shard_map(
        per_device, mesh=mesh, in_specs=in_specs, out_specs=out_specs, check_vma=False
    )
```

```python
import functools

import jax
import jax.numpy as jnp
from jax import lax
from jax.experimental import pallas as pl
from jax.experimental.pallas import tpu as pltpu
from jax.sharding import PartitionSpec as P

MESH = pl.DeviceIdType.MESH
BF = jnp.bfloat16
F32 = jnp.float32

D = 1408
H = 16
HD = 88
PD = 384
PH = 1536
BLK = 64
ROWS = 128
GRP = 384
HS = 256
QM = 512
LOG2E = 1.4426950408889634
NT = (((1,), (1,)), ((), ()))
TN = (((0,), (0,)), ((), ()))

gelu_coef = 0.7978845608
gelu_cube = 0.044715


def mm(a, b, dims=(((1,), (0,)), ((), ()))):
    return lax.dot_general(a, b, dims, preferred_element_type=F32)


def layer_norm(values):
    center = values - jnp.mean(values, axis=-1, keepdims=True)
    variance = jnp.mean(center * center, axis=-1, keepdims=True)
    factor = lax.rsqrt(variance + 1e-06)
    return center * factor, factor


def gelu_parts(values):
    inner = gelu_coef * (values + gelu_cube * values * values * values)
    tangent = jnp.tanh(inner)
    value = 0.5 * values * (1.0 + tangent)
    slope = 0.5 * (1.0 + tangent) + 0.5 * values * (1.0 - tangent * tangent) * gelu_coef * (
        1.0 + 3.0 * gelu_cube * values * values
    )
    return value, slope


class Here:
    def __init__(self):
        self.seq = lax.axis_index("seq")
        self.x = lax.axis_index("batch")
        self.k = lax.rem(self.seq, 2)
        self.y = lax.rem(lax.div(self.seq, 2), 4)
        self.z = lax.div(self.seq, 8)

    def at(self, x=None, y=None, z=None, k=None):
        x = self.x if x is None else x
        y = self.y if y is None else y
        z = self.z if z is None else z
        k = self.k if k is None else k
        return {"seq": (z * 4 + y) * 2 + k, "batch": x}

    def step(self, axis, by):
        pos = lax.rem(getattr(self, axis) + by, 4)
        return pos, self.at(**{axis: pos})

    def partner(self):
        return self.at(k=1 - self.k)


class Net:
    def __init__(self, here, send, recv):
        self.dev, self.send, self.recv = here.partner(), send, recv
        self.sends = self.recvs = 0

    def out(self):
        self.sends += 1
        return self.send.at[self.sends - 1]

    def into(self):
        self.recvs += 1
        return self.recv.at[self.recvs - 1]

    def copy(self, src, dst, dev, send_sem, recv_sem):
        return pltpu.make_async_remote_copy(
            src_ref=src, dst_ref=dst, send_sem=send_sem, recv_sem=recv_sem,
            device_id=dev, device_id_type=MESH,
        )

    def sent(self, sem, view):
        self.copy(view, view, self.dev, sem, sem).wait_send()

    def came(self, sem, view):
        self.copy(view, view, self.dev, sem, sem).wait_recv()


class RingGather:
    def __init__(self, net, here, axis, own, view, rows_a, rows, three):
        self.net, self.view, self.ra, self.rows, self.three = net, view, rows_a, rows, three
        self.me = getattr(here, axis)
        self.right_pos, self.right = here.step(axis, 1)
        self.left_pos, self.left = here.step(axis, 3)
        self.far_pos, _ = here.step(axis, 2)
        a, b = pl.ds(0, rows_a), pl.ds(rows_a, rows - rows_a)
        self.left_in, self.right_in, self.near_in, self.far_in = (net.into() for _ in range(4))
        self.done_out = s = net.out()
        mine_a, mine_b = self.part(self.me, 0), self.part(self.me, 1)
        self.copies = (
            net.copy(own.at[a], mine_a, self.right, s, self.left_in),
            net.copy(own.at[b], mine_b, self.left, s, self.right_in),
            net.copy(own.at[b], mine_b, self.right, s, self.near_in),
            net.copy(own.at[a], mine_a, self.left, s, self.near_in),
        )
        from_left, from_right = self.part(self.left_pos, 0), self.part(self.right_pos, 1)
        self.on = (
            net.copy(from_left, from_left, self.right, s, self.far_in),
            net.copy(from_right, from_right, self.left, s, self.far_in),
        )

    def part(self, pos, part):
        if part == 0:
            return self.view(pos, 0, self.ra)
        return self.view(pos, self.ra, self.rows - self.ra)

    def whole(self, pos):
        return self.view(pos, 0, self.rows)

    def start(self):
        for c in self.copies:
            c.start()

    def forward(self):
        self.net.came(self.left_in, self.part(self.left_pos, 0))
        self.on[0].start()
        self.net.came(self.right_in, self.part(self.right_pos, 1))
        self.on[1].start()

    def near(self):
        self.net.came(self.near_in, self.whole(self.me))

    def far(self):
        self.net.came(self.far_in, self.whole(self.me))

    def drain(self):
        self.net.sent(self.done_out, self.three)


class Mirror:
    def __init__(self, net, here, gather, own, total, groups):
        self.net, self.total = net, total
        self.done_out = net.out()
        self.ins = [(net.into(), view) for _, view in groups]
        sem_of = {n: self.ins[i][0] for i, (ns, _) in enumerate(groups) for n in ns}
        blocks = [] if own is None else [(own, gather.whole(gather.me))]
        for pos in (gather.left_pos, gather.right_pos, gather.far_pos):
            blocks.append((gather.whole(pos), gather.whole(pos)))
        self.copies = [
            net.copy(src, dst, here.partner(), self.done_out, sem_of[n])
            for n, (src, dst) in enumerate(blocks)
        ]

    def start(self, which):
        for i in which:
            self.copies[i].start()

    def wait_recv(self, group=0):
        self.net.came(*self.ins[group])

    def drain(self):
        self.net.sent(self.done_out, self.total)


class Halves:
    def __init__(self, net, here, gather, other, axis, three, six, nine):
        self.net, self.gather, self.other = net, gather, other
        self.three, self.six, self.nine = three, six, nine
        self.right, self.left = here.step(axis, 1)[1], here.step(axis, 3)[1]
        self.partner = here.partner()
        self.done_out, self.half_in, self.done_in = net.out(), net.into(), net.into()

    def pass_on(self, src, dev, sem):
        self.net.copy(src, src, dev, self.done_out, sem).start()

    def hand_out(self, places):
        g = self.gather
        for pos in places:
            self.pass_on(g.whole(pos), self.partner, self.done_in)
            self.pass_on(g.part(pos, 0), self.right, self.half_in)
            self.pass_on(g.part(pos, 1), self.left, self.half_in)

    def near(self):
        self.gather.near()
        self.hand_out([self.gather.left_pos, self.gather.right_pos])

    def far(self):
        self.gather.far()
        self.hand_out([self.gather.far_pos])

    def hand_in(self):
        g = self.gather
        self.net.came(self.half_in, self.three)
        for pos in (g.left_pos, g.right_pos, g.far_pos):
            self.pass_on(self.other(pos), self.partner, self.done_in)

    def done(self):
        self.net.came(self.done_in, self.six)

    def drain(self):
        self.gather.drain()
        self.net.sent(self.done_out, self.nine)


def spread(rows, cols):
    i = lax.broadcasted_iota(jnp.int32, (rows, cols), 0)
    j = lax.broadcasted_iota(jnp.int32, (rows, cols), 1)
    lane = j % 128
    return jnp.where((lane < HD) & (i == (j // 128) * HD + lane), 1.0, 0.0).astype(BF)


def gather_spread(rows, cols):
    i = lax.broadcasted_iota(jnp.int32, (rows, cols), 0)
    j = lax.broadcasted_iota(jnp.int32, (rows, cols), 1)
    lane = i % 128
    return jnp.where((lane < HD) & (j == (i // 128) * HD + lane), 1.0, 0.0).astype(BF)


FAN = (0, 1, 3, 2)


def step_kernel(
    tok_ref, qkv_hbm, stream_hbm, ow_ref, up_hbm, down_hbm, proj_hbm, mask_hbm, owner_hbm,
    out_ref,
    mask_ref, owner_ref, win, wsend, st, spsend,
    tokbuf, normed, wbuf, sbuf, outq, qpack, kpack, vpack,
    qbuf, kbuf, vbuf, wout, up_ref, down_ref, proj_ref,
    acc, atts, att, pred, mnorm, rstdb, ups_ref, pds_ref, nall, hid, slope, gm, gmall, part, land,
    send, recv, asend, arecv, gsend, grecv, local,
):
    here = Here()
    net = Net(here, send, recv)
    peers = [here.step(a, s)[1] for a in ("x", "y", "z") for s in (1, 3)] + [here.partner(), here.step("z", 2)[1]]
    barrier = pltpu.get_barrier_semaphore()
    for dev in peers:
        pl.semaphore_signal(barrier, inc=1, device_id=dev, device_id_type=MESH)

    count = [0]

    def fetch(src, dst):
        c = pltpu.make_async_copy(src, dst, local.at[count[0]])
        count[0] += 1
        c.start()
        return c

    first = jnp.minimum(128 * lax.div(11 * here.y, 4), 896)
    skip = 352 * here.y - first
    win_in = {
        t: fetch(qkv_hbm.at[:, pl.ds(pl.multiple_of(t * D + first, 128), 512)], win.at[t])
        for t in (1, 2, 0)
    }
    def rows_at(ref, stride, base=0):
        return lambda pos, skip, n: ref.at[pl.ds(pl.multiple_of(pos * stride + base + skip, 16), n)]

    gt = RingGather(
        net, here, "y", tok_ref, rows_at(tokbuf, 128), 64, 128,
        tokbuf.at[pl.ds(0, 384)],
    )
    k_half = pl.ds(pl.multiple_of(176 * here.k, 16), 176)
    gw = [
        RingGather(
            net, here, "x", wsend.at[t, k_half], rows_at(wbuf.at[t], 352, 176 * here.k), 96, 176,
            wbuf.at[t, pl.ds(0, 528)],
        )
        for t in range(3)
    ]
    mw = [Mirror(net, here, g, None, g.three, [((0, 1, 2), g.three)]) for g in gw]
    gs = RingGather(
        net, here, "x", spsend, rows_at(sbuf.at[here.k], 256), 128, 256, sbuf.at[0, pl.ds(0, 768)]
    )
    ms = Mirror(net, here, gs, spsend, sbuf.at[0], [((0, 1, 2, 3), sbuf.at[0])])
    part_rows = pl.multiple_of(((here.y % 2) * 2 + here.k) * 96, 96)
    other_rows = pl.multiple_of(((1 - here.y % 2) * 2 + here.k) * 96, 96)
    go = RingGather(
        net, here, "x", wout.at[here.x, pl.ds(part_rows, 96)],
        lambda pos, skip, n: wout.at[pos, pl.ds(pl.multiple_of(part_rows + skip, 16), n)], 48, 96,
        wout.at[pl.ds(0, 3), pl.ds(0, 96)],
    )
    ho = Halves(
        net, here, go, lambda pos: wout.at[pos, pl.ds(other_rows, 96)], "y",
        *[wout.at[pl.ds(0, 3), pl.ds(0, 96 * n)] for n in (1, 2, 3)],
    )
    tok_in = fetch(tok_ref, gt.whole(here.y))
    owner_in = fetch(owner_hbm, owner_ref)
    mask_in = fetch(mask_hbm, mask_ref)
    st_in = fetch(stream_hbm, st)
    up_in = fetch(up_hbm, up_ref)
    down_in = fetch(down_hbm, down_ref)
    own_o = fetch(ow_ref, wout.at[here.x, pl.ds(0, 352)])
    proj_in = fetch(proj_hbm, proj_ref)
    wout[here.x, pl.ds(352, 32), :] = jnp.zeros((32, D), BF)

    i = lax.broadcasted_iota(jnp.int32, (512, GRP), 0)
    j = lax.broadcasted_iota(jnp.int32, (512, GRP), 1)
    columns = jnp.where((i == j + skip) & (j < 352), 1.0, 0.0).astype(BF)

    def cut(t):
        win_in[t].wait()
        exact = mm(win[t], columns).astype(BF)
        wsend[t] = exact
        wbuf[t, pl.ds(pl.multiple_of(352 * here.x, 16), 352), :] = exact

    def norm_block(slot, pos):
        value = layer_norm(gt.whole(pos)[...].astype(F32))[0].astype(BF)
        normed[slot * 128:(slot + 1) * 128, :] = value

    first_block = lax.div(here.seq, 2) * 4

    def owner(c, k, b):
        return owner_ref[c, first_block + 2 * k + b]

    cut(1)
    pl.semaphore_wait(barrier, len(peers))
    gt.start()
    gw[1].start()
    cut(2)
    gw[2].start()
    cut(0)
    tok_in.wait()
    norm_block(0, here.y)
    gw[1].forward()
    gw[0].start()
    st_in.wait()
    owner_in.wait()
    mask_in.wait()
    for c in range(4):
        block = jnp.where(owner(c, here.k, 0) == here.x, 0, 1)
        rows = st[c, pl.ds(block * 64, 64), :]
        spsend[c * 64:(c + 1) * 64, :] = rows
        sbuf[here.k, pl.ds(pl.multiple_of(here.x * 256 + c * 64, 64), 64), :] = rows
    up_in.wait()
    down_in.wait()
    i = lax.broadcasted_iota(jnp.int32, (PH, HS), 0)
    j = lax.broadcasted_iota(jnp.int32, (PH, HS), 1)
    unit = ((j // 16) * 2 + here.k) * 48 + here.x * 12 + j % 16
    select = jnp.where((j % 16 < 12) & (i == unit), 1.0, 0.0).astype(BF)
    ups_ref[...] = mm(up_ref[...], select).astype(BF)
    pds_ref[...] = mm(select, down_ref[...], TN).astype(BF)

    gt.forward()
    gw[1].near()
    mw[1].start([0, 1])
    gw[2].forward()
    gw[2].near()
    mw[2].start([0, 1])
    gw[1].far()
    mw[1].start([2])
    gw[0].forward()
    own_o.wait()
    go.start()
    gt.near()
    norm_block(1, gt.right_pos)
    norm_block(2, gt.left_pos)
    mw[1].wait_recv()

    zr, right = here.step("z", 1)
    zl, left = here.step("z", 3)
    zf, across = here.step("z", 2)
    bufs = (qpack, kpack.at[here.k], vpack.at[here.k])
    pad = spread(GRP, 512)
    lane = lax.broadcasted_iota(jnp.int32, (1, 512), 1) % 128
    ones = jnp.where(lane >= HD, 1.0, 0.0)
    slot_of = lax.broadcasted_iota(jnp.int32, (1, GRP), 1) // HD
    head_out = [net.out() for _ in range(3)]
    near_in = [net.into() for _ in range(3)]
    far_in = [net.into(), net.into()]
    pass_out = net.out()
    pass_in = [net.into() for _ in range(3)]
    own = {}

    def pass_head(t, src, pos, group):
        buf = bufs[t]
        src = buf.at[pos] if src is None else src
        net.copy(src, buf.at[pos], here.partner(), pass_out, pass_in[group]).start()

    packed = {}

    def project(t, g0, n):
        rows = mm(normed[g0 * 128:(g0 + n) * 128], wbuf[t])
        if t == 0:
            rows = rows * (LOG2E / HD**0.5)
        for h in range(4):
            value = packed.get((t, h), jnp.zeros((128, GRP), F32))
            for g in range(g0, g0 + n):
                block = rows[(g - g0) * 128:(g - g0 + 1) * 128]
                turn = (HD * (g - h)) % GRP
                if turn:
                    block = pltpu.roll(block, turn, 1)
                value = jnp.where(slot_of == g, block, value)
            if g0 == 0 and n < 4:
                packed[t, h] = value
                outq[t, h, :, 0:256] = value[:, 0:256].astype(BF)
            elif g0 == 0:
                outq[t, h] = value.astype(BF)
            else:
                outq[t, h, :, 256:GRP] = value[:, 256:GRP].astype(BF)
        if g0 == 0:
            at = pl.ds(0, GRP if n == 4 else 256)
        else:
            at = pl.ds(256, 128)
        for pos, dev in ((zr, right), (zl, left)):
            net.copy(
                outq.at[t, pos, :, at], bufs[t].at[here.z, :, at], dev, head_out[t], near_in[t]
            ).start()
        if g0 + n == 4:
            net.copy(
                outq.at[t, zf], bufs[t].at[here.z], across, head_out[t], far_in[1 if t else 0]
            ).start()
            own[t] = fetch(outq.at[t, here.z], bufs[t].at[here.z])
            if t:
                pass_head(t, outq.at[t, here.z], here.z, 0)

    def widen(block):
        return mm(block, pad)

    def unpack_q(dz):
        z = lax.rem(here.z + dz, 4)
        wide = widen(qpack[z]).astype(BF)
        for g in range(4):
            qbuf[dz, g * 128:(g + 1) * 128, :] = wide[:, g * 128:(g + 1) * 128]

    def unpack_kv(dz, cores=(0, 1)):
        z = lax.rem(here.z + dz, 4)
        for c in cores:
            core = 1 - here.k if c else here.k
            for pack_ref, buf, extra in ((kpack, kbuf, None), (vpack, vbuf, ones)):
                wide = widen(pack_ref[core, z])
                if extra is not None:
                    wide = wide + extra
                wide = wide.astype(BF)
                for g in range(4):
                    buf[c, dz, g * 128:(g + 1) * 128, :] = wide[:, g * 128:(g + 1) * 128]

    project(1, 0, 3)
    gw[0].near()
    mw[0].start([0, 1])
    gt.far()
    norm_block(3, gt.far_pos)
    gw[2].far()
    mw[2].start([2])
    project(1, 3, 1)
    mw[2].wait_recv()
    project(2, 0, 4)
    gw[0].far()
    mw[0].start([2])
    mw[0].wait_recv()
    go.forward()
    gs.start()
    ms.start([0])
    project(0, 0, 4)

    def pair(dq, dk, first, cores=(0, 1)):
        for half in range(512 // QM):
            at = slice(half * QM, (half + 1) * QM)
            q = qbuf[dq, at, :]
            total = None
            for c in cores:
                p = jnp.exp2(mm(q, kbuf[c, dk], NT)).astype(BF)
                term = mm(p, vbuf[c, dk])
                total = term if total is None else total + term
            acc[dq, at, :] = total if first else acc[dq, at, :] + total

    head = here.y * 4 + here.z

    def back(slot):
        zc = lax.rem(here.z + slot // 4, 4)
        yc = lax.rem(here.y + FAN[slot % 4], 4)
        return pltpu.make_async_remote_copy(
            src_ref=atts.at[slot], dst_ref=att.at[head],
            send_sem=asend.at[0], recv_sem=arecv.at[here.y],
            device_id=here.at(z=zc, y=yc), device_id_type=MESH,
        )

    def finish(dq):
        value = acc[dq]
        value = (value / value[:, HD:HD + 1]).astype(BF)
        for n in range(4):
            slot = dq * 4 + n
            atts[slot] = value[n * 128:(n + 1) * 128]
            if slot:
                back(slot).start()

    for t in (1, 2, 0):
        own[t].wait()
    unpack_q(0)
    unpack_kv(0, (0,))
    pair(0, 0, True, (0,))
    net.came(pass_in[0], kpack.at[0, pl.ds(0, 2)])
    unpack_kv(0, (1,))
    pair(0, 0, False, (1,))
    for t in (1, 2):
        net.came(near_in[t], kpack.at[0, pl.ds(0, 2)])
        pass_head(t, None, zl, 1)
        pass_head(t, None, zr, 1)
    ho.near()
    for dk in (1, 3):
        unpack_kv(dk, (0,))
        pair(0, dk, False, (0,))
    net.came(far_in[1], kpack.at[0, pl.ds(0, 2)])
    for t in (1, 2):
        pass_head(t, None, zf, 2)
    net.came(pass_in[1], kpack.at[0])
    for dk in (1, 3):
        unpack_kv(dk, (1,))
        pair(0, dk, False, (1,))
    ho.far()
    net.came(near_in[0], kpack.at[0, pl.ds(0, 2)])
    unpack_q(1)
    unpack_q(3)
    for dk in (0, 1, 3):
        pair(1, dk, dk == 0)
    gs.forward()
    net.came(pass_in[2], kpack.at[0, pl.ds(0, 2)])
    unpack_kv(2)
    pair(1, 2, False)
    finish(1)
    net.came(far_in[0], kpack.at[0, 0])
    gs.near()
    ms.start([1, 2])
    unpack_q(2)
    for dk in (2, 0, 1, 3):
        pair(2, dk, dk == 2)
    finish(2)
    gs.far()
    ms.start([3])
    for dk in (0, 1, 2, 3):
        pair(3, dk, dk == 0)
    finish(3)
    ho.hand_in()
    pair(0, 2, False)
    finish(0)
    own_a = fetch(atts.at[0], att.at[head])

    proj_in.wait()
    ms.wait_recv()
    stream = jnp.concatenate(
        [
            sbuf[here.k, pl.ds(owner(here.x, here.k, b) * 256 + here.x * 64, 64), :]
            for b in range(2)
        ],
        axis=0,
    ).astype(F32)
    normed_own = layer_norm(stream)[0].astype(BF)
    hidden = gelu_parts(mm(normed_own, up_ref[...]))[0].astype(BF)
    mixed = stream + mm(hidden, down_ref[...])
    mixed_norm, rstd = layer_norm(mixed)
    mnorm[...] = mixed_norm
    rstdb[...] = jnp.broadcast_to(rstd, (ROWS, 128))
    pred[...] = mm(mixed_norm.astype(BF), proj_ref[...])

    def share(slot):
        c = lax.rem(here.x + FAN[slot], 4)
        for k in range(2):
            at = slice((slot * 2 + k) * 128, (slot * 2 + k + 1) * 128)
            rows = jnp.concatenate(
                [sbuf[k, pl.ds(owner(c, k, b) * 256 + c * 64, 64), :] for b in range(2)],
                axis=0,
            )
            nv = layer_norm(rows.astype(F32))[0].astype(BF)
            nall[at, :] = nv
            value, deriv = gelu_parts(mm(nv, ups_ref[...]))
            hid[at, :] = value.astype(BF)
            slope[at, :] = deriv

    share(0)
    share(1)
    ho.done()
    own_a.wait()
    pack = gather_spread(512, GRP)
    total = gt.whole(here.y)[...].astype(F32)
    for dy in (0, 1, 3, 2):
        group = lax.rem(here.y + dy, 4)
        net.came(arecv.at[group], att.at[pl.ds(0, 4 if dy else 3)])
        wide = jnp.concatenate([att[group * 4 + h] for h in range(4)], axis=1)
        total = total + mm(mm(wide, pack).astype(BF), wout[group])
    target = layer_norm(total)[0].astype(BF).astype(F32)
    masked = mask_ref[pl.ds(here.x, 1), :]
    lives = []
    for b in range(2):
        hit = jnp.where(masked == here.seq * 2 + b, 1.0, 0.0)
        lives.append(jnp.broadcast_to(jnp.max(hit, axis=1, keepdims=True), (BLK, 1)))
    live = jnp.concatenate(lives, axis=0) / float(4 * masked.shape[1])
    grad_pred = ((pred[...] - target) * live).astype(BF)
    grad_norm = mm(grad_pred, proj_ref[...], NT)
    mixed_norm = mnorm[...]
    first_mean = jnp.mean(grad_norm, axis=-1, keepdims=True)
    second_mean = jnp.mean(grad_norm * mixed_norm, axis=-1, keepdims=True)
    grad = (rstdb[:, 0:1] * (grad_norm - first_mean - mixed_norm * second_mean)).astype(BF)
    gm[...] = grad
    gmall[here.k, pl.ds(pl.multiple_of(here.x * 128, 128), 128), :] = grad

    gg = RingGather(net, here, "x", gm, rows_at(gmall.at[here.k], 128), 64, 128, gmall.at[0, pl.ds(0, 384)])
    mg = Mirror(
        net, here, gg, gm, gmall.at[0],
        [((0, 1, 2), gmall.at[0, pl.ds(0, 384)]), ((3,), gmall.at[0, pl.ds(0, 128)])],
    )
    gg.start()
    mg.start([0])
    share(2)
    gg.forward()
    share(3)
    gg.near()
    mg.start([1, 2])
    mg.wait_recv(0)

    def grads(slots):
        places = [(gg.me, gg.right_pos, gg.left_pos, gg.far_pos)[n] for n in slots]
        rows = [
            gmall[k, pl.ds(pl.multiple_of(pos * 128, 128), 128), :]
            for pos in places for k in range(2)
        ]
        grad_mixed = jnp.concatenate(rows, axis=0)
        at = slice(slots[0] * 256, (slots[-1] + 1) * 256)
        down = mm(hid[at, :], grad_mixed, TN)
        grad_hidden = mm(grad_mixed, pds_ref[...], NT)
        grad_pre = (grad_hidden * slope[at, :]).astype(BF)
        return mm(grad_pre, nall[at, :], TN), down

    up_near, down_near = grads((0, 1, 2))
    gg.far()
    mg.start([3])
    mg.wait_recv(1)
    grad_up, grad_down = grads((3,))
    grad_up = grad_up + up_near
    grad_down = grad_down + down_near
    grad_up = grad_up.reshape(16, 2, 8, PD)
    grad_down = grad_down.reshape(16, 2, 8, PD)
    low = lax.broadcasted_iota(jnp.int32, (8, PD), 0) < 4
    part[:, :, 0:PD] = grad_up[:, 0].astype(BF)
    part[:, :, PD:2 * PD] = grad_down[:, 0].astype(BF)
    for d in range(16):
        both = jnp.where(low, grad_up[d, 1], pltpu.roll(grad_down[d, 1], 4, 0))
        part[d, :, 2 * PD:3 * PD] = both.astype(BF)

    me = here.z * 4 + here.y
    for d in range(1, 16):
        to = lax.rem(me + d, 16)
        net.copy(
            part.at[to], land.at[me], here.at(z=lax.div(to, 4), y=lax.rem(to, 4)),
            gsend.at[0], grecv.at[0],
        ).start()
    for c in [gt, gs, ho, gg, ms, mg] + gw + mw:
        c.drain()
    for t in range(3):
        net.sent(head_out[t], outq.at[t, pl.ds(0, 3)])
    net.sent(pass_out, kpack)
    net.sent(asend.at[0], atts.at[pl.ds(0, 15)])
    total = part[me].astype(F32)
    net.came(grecv.at[0], land.at[pl.ds(0, 15)])
    for d in range(1, 16):
        total = total + land[lax.rem(me + d, 16)].astype(F32)
    out_ref[0:8, :] = total[:, 0:2 * PD]
    out_ref[8:12, 0:PD] = total[0:4, 2 * PD:3 * PD]
    out_ref[8:12, PD:2 * PD] = total[4:8, 2 * PD:3 * PD]
    net.sent(gsend.at[0], part.at[pl.ds(0, 15)])


VM = pl.BlockSpec(memory_space=pltpu.VMEM)
ANY = pl.BlockSpec(memory_space=pl.ANY)
DMA = pltpu.SemaphoreType.DMA


def sds(shape, dtype):
    return jax.ShapeDtypeStruct(shape, dtype)


def params(cid):
    return pltpu.CompilerParams(
        collective_id=cid, has_side_effects=True, vmem_limit_bytes=60 * 1024 * 1024
    )


def per_device(
    tokens, qkv_weight, out_weight, mask_blocks, owner_map, pred_stream, pred_up, pred_down,
    pred_proj,
):
    share = pl.pallas_call(
        step_kernel,
        out_shape=sds((12, 2 * PD), F32),
        in_specs=[ANY] * 9,
        out_specs=VM,
        scratch_shapes=[
            pltpu.VMEM((4, 56), jnp.int32), pltpu.SMEM((4, 64), jnp.int32),
            pltpu.VMEM((3, 352, 512), BF), pltpu.VMEM((3, 352, GRP), BF),
            pltpu.VMEM((4, ROWS, PD), BF), pltpu.VMEM((4 * BLK, PD), BF),
            pltpu.VMEM((512, D), BF), pltpu.VMEM((512, D), BF), pltpu.VMEM((3, D, GRP), BF),
            pltpu.VMEM((2, 1024, PD), BF), pltpu.VMEM((3, 4, 128, GRP), BF),
            pltpu.VMEM((4, 128, GRP), BF), pltpu.VMEM((2, 4, 128, GRP), BF),
            pltpu.VMEM((2, 4, 128, GRP), BF),
            pltpu.VMEM((4, 512, 128), BF), pltpu.VMEM((2, 4, 512, 128), BF),
            pltpu.VMEM((2, 4, 512, 128), BF),
            pltpu.VMEM((4, GRP, D), BF), pltpu.VMEM((PD, PH), BF), pltpu.VMEM((PH, PD), BF),
            pltpu.VMEM((PD, D), BF), pltpu.VMEM((4, 512, 128), F32),
            pltpu.VMEM((16, 128, 128), BF), pltpu.VMEM((16, 128, 128), BF),
            pltpu.VMEM((ROWS, D), F32), pltpu.VMEM((ROWS, PD), F32), pltpu.VMEM((ROWS, 128), F32),
            pltpu.VMEM((PD, HS), BF), pltpu.VMEM((HS, PD), BF), pltpu.VMEM((1024, PD), BF),
            pltpu.VMEM((1024, HS), BF), pltpu.VMEM((1024, HS), F32), pltpu.VMEM((ROWS, PD), BF),
            pltpu.VMEM((2, 512, PD), BF), pltpu.VMEM((16, 8, 3 * PD), BF),
            pltpu.VMEM((16, 8, 3 * PD), BF),
            DMA((17,)), DMA((44,)), DMA((1,)), DMA((4,)), DMA((1,)), DMA((1,)), DMA((15,)),
        ],
        compiler_params=params(1),
        name="step",
    )(
        tokens[0], qkv_weight, pred_stream[0], out_weight, pred_up, pred_down, pred_proj,
        mask_blocks, owner_map,
    )
    return share[:, :PD].T, share[:, PD:]


def solution(mesh):
    in_specs = (
        P("batch", "seq", None),
        P("batch", None),
        P("batch", None),
        P(),
        P(),
        P("batch", None, "seq", None),
        P(),
        P(),
        P(),
    )
    out_specs = (P(None, ("seq", "batch")), P(("seq", "batch"), None))
    return jax.shard_map(
        per_device, mesh=mesh, in_specs=in_specs, out_specs=out_specs, check_vma=False
    )
```

```python
import functools

import jax
import jax.numpy as jnp
from jax import lax
from jax.experimental import pallas as pl
from jax.experimental.pallas import tpu as pltpu
from jax.sharding import PartitionSpec as P

MESH = pl.DeviceIdType.MESH
BF = jnp.bfloat16
F32 = jnp.float32

D = 1408
H = 16
HD = 88
PD = 384
PH = 1536
BLK = 64
ROWS = 128
GRP = 384
HS = 256
QM = 512
LOG2E = 1.4426950408889634
NT = (((1,), (1,)), ((), ()))
TN = (((0,), (0,)), ((), ()))

gelu_coef = 0.7978845608
gelu_cube = 0.044715


def mm(a, b, dims=(((1,), (0,)), ((), ()))):
    return lax.dot_general(a, b, dims, preferred_element_type=F32)


def layer_norm(values):
    center = values - jnp.mean(values, axis=-1, keepdims=True)
    variance = jnp.mean(center * center, axis=-1, keepdims=True)
    factor = lax.rsqrt(variance + 1e-06)
    return center * factor, factor


def gelu_parts(values):
    inner = gelu_coef * (values + gelu_cube * values * values * values)
    tangent = jnp.tanh(inner)
    value = 0.5 * values * (1.0 + tangent)
    slope = 0.5 * (1.0 + tangent) + 0.5 * values * (1.0 - tangent * tangent) * gelu_coef * (
        1.0 + 3.0 * gelu_cube * values * values
    )
    return value, slope


class Here:
    def __init__(self):
        self.seq = lax.axis_index("seq")
        self.x = lax.axis_index("batch")
        self.k = lax.rem(self.seq, 2)
        self.y = lax.rem(lax.div(self.seq, 2), 4)
        self.z = lax.div(self.seq, 8)

    def at(self, x=None, y=None, z=None, k=None):
        x = self.x if x is None else x
        y = self.y if y is None else y
        z = self.z if z is None else z
        k = self.k if k is None else k
        return {"seq": (z * 4 + y) * 2 + k, "batch": x}

    def step(self, axis, by):
        pos = lax.rem(getattr(self, axis) + by, 4)
        return pos, self.at(**{axis: pos})

    def partner(self):
        return self.at(k=1 - self.k)


class Net:
    def __init__(self, here, send, recv):
        self.dev, self.send, self.recv = here.partner(), send, recv
        self.sends = self.recvs = 0

    def out(self):
        self.sends += 1
        return self.send.at[self.sends - 1]

    def into(self):
        self.recvs += 1
        return self.recv.at[self.recvs - 1]

    def copy(self, src, dst, dev, send_sem, recv_sem):
        return pltpu.make_async_remote_copy(
            src_ref=src, dst_ref=dst, send_sem=send_sem, recv_sem=recv_sem,
            device_id=dev, device_id_type=MESH,
        )

    def sent(self, sem, view):
        self.copy(view, view, self.dev, sem, sem).wait_send()

    def came(self, sem, view):
        self.copy(view, view, self.dev, sem, sem).wait_recv()


class RingGather:
    def __init__(self, net, here, axis, own, view, rows_a, rows, three):
        self.net, self.view, self.ra, self.rows, self.three = net, view, rows_a, rows, three
        self.me = getattr(here, axis)
        self.right_pos, self.right = here.step(axis, 1)
        self.left_pos, self.left = here.step(axis, 3)
        self.far_pos, _ = here.step(axis, 2)
        a, b = pl.ds(0, rows_a), pl.ds(rows_a, rows - rows_a)
        self.left_in, self.right_in, self.near_in, self.far_in = (net.into() for _ in range(4))
        self.done_out = s = net.out()
        mine_a, mine_b = self.part(self.me, 0), self.part(self.me, 1)
        self.copies = (
            net.copy(own.at[a], mine_a, self.right, s, self.left_in),
            net.copy(own.at[b], mine_b, self.left, s, self.right_in),
            net.copy(own.at[b], mine_b, self.right, s, self.near_in),
            net.copy(own.at[a], mine_a, self.left, s, self.near_in),
        )
        from_left, from_right = self.part(self.left_pos, 0), self.part(self.right_pos, 1)
        self.on = (
            net.copy(from_left, from_left, self.right, s, self.far_in),
            net.copy(from_right, from_right, self.left, s, self.far_in),
        )

    def part(self, pos, part):
        if part == 0:
            return self.view(pos, 0, self.ra)
        return self.view(pos, self.ra, self.rows - self.ra)

    def whole(self, pos):
        return self.view(pos, 0, self.rows)

    def start(self):
        for c in self.copies:
            c.start()

    def forward(self):
        self.net.came(self.left_in, self.part(self.left_pos, 0))
        self.on[0].start()
        self.net.came(self.right_in, self.part(self.right_pos, 1))
        self.on[1].start()

    def near(self):
        self.net.came(self.near_in, self.whole(self.me))

    def far(self):
        self.net.came(self.far_in, self.whole(self.me))

    def drain(self):
        self.net.sent(self.done_out, self.three)


class Mirror:
    def __init__(self, net, here, gather, own, total, groups):
        self.net, self.total = net, total
        self.done_out = net.out()
        self.ins = [(net.into(), view) for _, view in groups]
        sem_of = {n: self.ins[i][0] for i, (ns, _) in enumerate(groups) for n in ns}
        blocks = [] if own is None else [(own, gather.whole(gather.me))]
        for pos in (gather.left_pos, gather.right_pos, gather.far_pos):
            blocks.append((gather.whole(pos), gather.whole(pos)))
        self.copies = [
            net.copy(src, dst, here.partner(), self.done_out, sem_of[n])
            for n, (src, dst) in enumerate(blocks)
        ]

    def start(self, which):
        for i in which:
            self.copies[i].start()

    def wait_recv(self, group=0):
        self.net.came(*self.ins[group])

    def drain(self):
        self.net.sent(self.done_out, self.total)


class Halves:
    def __init__(self, net, here, gather, other, axis, three, six, nine):
        self.net, self.gather, self.other = net, gather, other
        self.three, self.six, self.nine = three, six, nine
        self.right, self.left = here.step(axis, 1)[1], here.step(axis, 3)[1]
        self.partner = here.partner()
        self.done_out, self.half_in, self.done_in = net.out(), net.into(), net.into()

    def pass_on(self, src, dev, sem):
        self.net.copy(src, src, dev, self.done_out, sem).start()

    def hand_out(self, places):
        g = self.gather
        for pos in places:
            self.pass_on(g.whole(pos), self.partner, self.done_in)
            self.pass_on(g.part(pos, 0), self.right, self.half_in)
            self.pass_on(g.part(pos, 1), self.left, self.half_in)

    def near(self):
        self.gather.near()
        self.hand_out([self.gather.left_pos, self.gather.right_pos])

    def far(self):
        self.gather.far()
        self.hand_out([self.gather.far_pos])

    def hand_in(self):
        g = self.gather
        self.net.came(self.half_in, self.three)
        for pos in (g.left_pos, g.right_pos, g.far_pos):
            self.pass_on(self.other(pos), self.partner, self.done_in)

    def done(self):
        self.net.came(self.done_in, self.six)

    def drain(self):
        self.gather.drain()
        self.net.sent(self.done_out, self.nine)


def spread(rows, cols):
    i = lax.broadcasted_iota(jnp.int32, (rows, cols), 0)
    j = lax.broadcasted_iota(jnp.int32, (rows, cols), 1)
    lane = j % 128
    return jnp.where((lane < HD) & (i == (j // 128) * HD + lane), 1.0, 0.0).astype(BF)


def gather_spread(rows, cols):
    i = lax.broadcasted_iota(jnp.int32, (rows, cols), 0)
    j = lax.broadcasted_iota(jnp.int32, (rows, cols), 1)
    lane = i % 128
    return jnp.where((lane < HD) & (j == (i // 128) * HD + lane), 1.0, 0.0).astype(BF)


FAN = (0, 1, 3, 2)


def step_kernel(
    tok_ref, qkv_hbm, stream_hbm, ow_ref, up_hbm, down_hbm, proj_hbm, mask_hbm, owner_hbm,
    out_ref,
    mask_ref, owner_ref, win, wsend, st, spsend,
    tokbuf, normed, wbuf, sbuf, outq, qpack, kpack, vpack,
    qbuf, kbuf, vbuf, wout, up_ref, down_ref, proj_ref,
    acc, atts, att, pred, mnorm, rstdb, ups_ref, pds_ref, nall, hid, slope, gm, gmall, part, land,
    send, recv, asend, arecv, gsend, grecv, local,
):
    here = Here()
    net = Net(here, send, recv)
    peers = [here.step(a, s)[1] for a in ("x", "y", "z") for s in (1, 3)] + [here.partner(), here.step("z", 2)[1]]
    barrier = pltpu.get_barrier_semaphore()
    for dev in peers:
        pl.semaphore_signal(barrier, inc=1, device_id=dev, device_id_type=MESH)

    count = [0]

    def fetch(src, dst):
        c = pltpu.make_async_copy(src, dst, local.at[count[0]])
        count[0] += 1
        c.start()
        return c

    first = jnp.minimum(128 * lax.div(11 * here.y, 4), 896)
    skip = 352 * here.y - first
    win_in = {
        t: fetch(qkv_hbm.at[:, pl.ds(pl.multiple_of(t * D + first, 128), 512)], win.at[t])
        for t in (1, 2, 0)
    }
    def rows_at(ref, stride, base=0):
        return lambda pos, skip, n: ref.at[pl.ds(pl.multiple_of(pos * stride + base + skip, 16), n)]

    gt = RingGather(
        net, here, "y", tok_ref, rows_at(tokbuf, 128), 64, 128,
        tokbuf.at[pl.ds(0, 384)],
    )
    k_half = pl.ds(pl.multiple_of(176 * here.k, 16), 176)
    gw = [
        RingGather(
            net, here, "x", wsend.at[t, k_half], rows_at(wbuf.at[t], 352, 176 * here.k), 96, 176,
            wbuf.at[t, pl.ds(0, 528)],
        )
        for t in range(3)
    ]
    mw = [Mirror(net, here, g, None, g.three, [((0, 1, 2), g.three)]) for g in gw]
    gs = RingGather(
        net, here, "x", spsend, rows_at(sbuf.at[here.k], 256), 128, 256, sbuf.at[0, pl.ds(0, 768)]
    )
    ms = Mirror(net, here, gs, spsend, sbuf.at[0], [((0, 1, 2, 3), sbuf.at[0])])
    part_rows = pl.multiple_of(((here.y % 2) * 2 + here.k) * 96, 96)
    other_rows = pl.multiple_of(((1 - here.y % 2) * 2 + here.k) * 96, 96)
    go = RingGather(
        net, here, "x", wout.at[here.x, pl.ds(part_rows, 96)],
        lambda pos, skip, n: wout.at[pos, pl.ds(pl.multiple_of(part_rows + skip, 16), n)], 48, 96,
        wout.at[pl.ds(0, 3), pl.ds(0, 96)],
    )
    ho = Halves(
        net, here, go, lambda pos: wout.at[pos, pl.ds(other_rows, 96)], "y",
        *[wout.at[pl.ds(0, 3), pl.ds(0, 96 * n)] for n in (1, 2, 3)],
    )
    tok_in = fetch(tok_ref, gt.whole(here.y))
    owner_in = fetch(owner_hbm, owner_ref)
    mask_in = fetch(mask_hbm, mask_ref)
    st_in = fetch(stream_hbm, st)
    up_in = fetch(up_hbm, up_ref)
    down_in = fetch(down_hbm, down_ref)
    own_o = fetch(ow_ref, wout.at[here.x, pl.ds(0, 352)])
    proj_in = fetch(proj_hbm, proj_ref)
    wout[here.x, pl.ds(352, 32), :] = jnp.zeros((32, D), BF)

    i = lax.broadcasted_iota(jnp.int32, (512, GRP), 0)
    j = lax.broadcasted_iota(jnp.int32, (512, GRP), 1)
    columns = jnp.where((i == j + skip) & (j < 352), 1.0, 0.0).astype(BF)

    def cut(t):
        win_in[t].wait()
        exact = mm(win[t], columns).astype(BF)
        wsend[t] = exact
        wbuf[t, pl.ds(pl.multiple_of(352 * here.x, 16), 352), :] = exact

    def norm_block(slot, pos):
        value = layer_norm(gt.whole(pos)[...].astype(F32))[0].astype(BF)
        normed[slot * 128:(slot + 1) * 128, :] = value

    first_block = lax.div(here.seq, 2) * 4

    def owner(c, k, b):
        return owner_ref[c, first_block + 2 * k + b]

    cut(1)
    pl.semaphore_wait(barrier, len(peers))
    gt.start()
    gw[1].start()
    cut(2)
    gw[2].start()
    cut(0)
    tok_in.wait()
    norm_block(0, here.y)
    gw[1].forward()
    gw[0].start()
    st_in.wait()
    owner_in.wait()
    mask_in.wait()
    for c in range(4):
        block = jnp.where(owner(c, here.k, 0) == here.x, 0, 1)
        rows = st[c, pl.ds(block * 64, 64), :]
        spsend[c * 64:(c + 1) * 64, :] = rows
        sbuf[here.k, pl.ds(pl.multiple_of(here.x * 256 + c * 64, 64), 64), :] = rows
    up_in.wait()
    down_in.wait()
    i = lax.broadcasted_iota(jnp.int32, (PH, HS), 0)
    j = lax.broadcasted_iota(jnp.int32, (PH, HS), 1)
    unit = ((j // 16) * 2 + here.k) * 48 + here.x * 12 + j % 16
    select = jnp.where((j % 16 < 12) & (i == unit), 1.0, 0.0).astype(BF)
    ups_ref[...] = mm(up_ref[...], select).astype(BF)
    pds_ref[...] = mm(select, down_ref[...], TN).astype(BF)

    gt.forward()
    gw[1].near()
    mw[1].start([0, 1])
    gw[2].forward()
    gw[2].near()
    mw[2].start([0, 1])
    gw[1].far()
    mw[1].start([2])
    gw[0].forward()
    own_o.wait()
    go.start()
    gt.near()
    norm_block(1, gt.right_pos)
    norm_block(2, gt.left_pos)
    mw[1].wait_recv()

    zr, right = here.step("z", 1)
    zl, left = here.step("z", 3)
    zf, across = here.step("z", 2)
    bufs = (qpack, kpack.at[here.k], vpack.at[here.k])
    pad = spread(GRP, 512)
    lane = lax.broadcasted_iota(jnp.int32, (1, 512), 1) % 128
    ones = jnp.where(lane >= HD, 1.0, 0.0)
    slot_of = lax.broadcasted_iota(jnp.int32, (1, GRP), 1) // HD
    head_out = [net.out() for _ in range(3)]
    near_in = [net.into() for _ in range(3)]
    far_in = [net.into(), net.into()]
    pass_out = net.out()
    pass_in = [net.into() for _ in range(3)]
    own = {}

    def pass_head(t, src, pos, group):
        buf = bufs[t]
        src = buf.at[pos] if src is None else src
        net.copy(src, buf.at[pos], here.partner(), pass_out, pass_in[group]).start()

    packed = {}

    def project(t, g0, n):
        rows = mm(normed[g0 * 128:(g0 + n) * 128], wbuf[t])
        if t == 0:
            rows = rows * (LOG2E / HD**0.5)
        for h in range(4):
            value = packed.get((t, h), jnp.zeros((128, GRP), F32))
            for g in range(g0, g0 + n):
                block = rows[(g - g0) * 128:(g - g0 + 1) * 128]
                turn = (HD * (g - h)) % GRP
                if turn:
                    block = pltpu.roll(block, turn, 1)
                value = jnp.where(slot_of == g, block, value)
            if g0 == 0 and n < 4:
                packed[t, h] = value
                outq[t, h, :, 0:256] = value[:, 0:256].astype(BF)
            elif g0 == 0:
                outq[t, h] = value.astype(BF)
            else:
                outq[t, h, :, 256:GRP] = value[:, 256:GRP].astype(BF)
        if g0 == 0:
            at = pl.ds(0, GRP if n == 4 else 256)
        else:
            at = pl.ds(256, 128)
        for pos, dev in ((zr, right), (zl, left)):
            net.copy(
                outq.at[t, pos, :, at], bufs[t].at[here.z, :, at], dev, head_out[t], near_in[t]
            ).start()
        if g0 + n == 4:
            net.copy(
                outq.at[t, zf], bufs[t].at[here.z], across, head_out[t], far_in[1 if t else 0]
            ).start()
            own[t] = fetch(outq.at[t, here.z], bufs[t].at[here.z])
            if t:
                pass_head(t, outq.at[t, here.z], here.z, 0)

    def widen(block):
        return mm(block, pad)

    def unpack_q(dz):
        z = lax.rem(here.z + dz, 4)
        wide = widen(qpack[z]).astype(BF)
        for g in range(4):
            qbuf[dz, g * 128:(g + 1) * 128, :] = wide[:, g * 128:(g + 1) * 128]

    def unpack_kv(dz, cores=(0, 1)):
        z = lax.rem(here.z + dz, 4)
        for c in cores:
            core = 1 - here.k if c else here.k
            for pack_ref, buf, extra in ((kpack, kbuf, None), (vpack, vbuf, ones)):
                wide = widen(pack_ref[core, z])
                if extra is not None:
                    wide = wide + extra
                wide = wide.astype(BF)
                for g in range(4):
                    buf[c, dz, g * 128:(g + 1) * 128, :] = wide[:, g * 128:(g + 1) * 128]

    project(1, 0, 3)
    gw[0].near()
    mw[0].start([0, 1])
    gt.far()
    norm_block(3, gt.far_pos)
    gw[2].far()
    mw[2].start([2])
    project(1, 3, 1)
    mw[2].wait_recv()
    gw[0].far()
    mw[0].start([2])
    project(2, 0, 4)
    mw[0].wait_recv()
    go.forward()
    gs.start()
    ms.start([0])
    project(0, 0, 4)

    def pair(dq, dk, first, cores=(0, 1)):
        for half in range(512 // QM):
            at = slice(half * QM, (half + 1) * QM)
            q = qbuf[dq, at, :]
            total = None
            for c in cores:
                p = jnp.exp2(mm(q, kbuf[c, dk], NT)).astype(BF)
                term = mm(p, vbuf[c, dk])
                total = term if total is None else total + term
            acc[dq, at, :] = total if first else acc[dq, at, :] + total

    head = here.y * 4 + here.z

    def back(slot):
        zc = lax.rem(here.z + slot // 4, 4)
        yc = lax.rem(here.y + FAN[slot % 4], 4)
        return pltpu.make_async_remote_copy(
            src_ref=atts.at[slot], dst_ref=att.at[head],
            send_sem=asend.at[0], recv_sem=arecv.at[here.y],
            device_id=here.at(z=zc, y=yc), device_id_type=MESH,
        )

    def finish(dq):
        value = acc[dq]
        value = (value / value[:, HD:HD + 1]).astype(BF)
        for n in range(4):
            slot = dq * 4 + n
            atts[slot] = value[n * 128:(n + 1) * 128]
            if slot:
                back(slot).start()

    for t in (1, 2, 0):
        own[t].wait()
    unpack_q(0)
    unpack_kv(0, (0,))
    pair(0, 0, True, (0,))
    net.came(pass_in[0], kpack.at[0, pl.ds(0, 2)])
    unpack_kv(0, (1,))
    pair(0, 0, False, (1,))
    for t in (1, 2):
        net.came(near_in[t], kpack.at[0, pl.ds(0, 2)])
        pass_head(t, None, zl, 1)
        pass_head(t, None, zr, 1)
    ho.near()
    for dk in (1, 3):
        unpack_kv(dk, (0,))
        pair(0, dk, False, (0,))
    net.came(far_in[1], kpack.at[0, pl.ds(0, 2)])
    for t in (1, 2):
        pass_head(t, None, zf, 2)
    net.came(pass_in[1], kpack.at[0])
    for dk in (1, 3):
        unpack_kv(dk, (1,))
        pair(0, dk, False, (1,))
    ho.far()
    net.came(near_in[0], kpack.at[0, pl.ds(0, 2)])
    unpack_q(1)
    unpack_q(3)
    for dk in (0, 1, 3):
        pair(1, dk, dk == 0)
    gs.forward()
    net.came(pass_in[2], kpack.at[0, pl.ds(0, 2)])
    unpack_kv(2)
    pair(1, 2, False)
    finish(1)
    net.came(far_in[0], kpack.at[0, 0])
    gs.near()
    ms.start([1, 2])
    unpack_q(2)
    for dk in (2, 0, 1, 3):
        pair(2, dk, dk == 2)
    finish(2)
    gs.far()
    ms.start([3])
    for dk in (0, 1, 2, 3):
        pair(3, dk, dk == 0)
    finish(3)
    ho.hand_in()
    pair(0, 2, False)
    finish(0)
    own_a = fetch(atts.at[0], att.at[head])

    proj_in.wait()
    ms.wait_recv()
    stream = jnp.concatenate(
        [
            sbuf[here.k, pl.ds(owner(here.x, here.k, b) * 256 + here.x * 64, 64), :]
            for b in range(2)
        ],
        axis=0,
    ).astype(F32)
    normed_own = layer_norm(stream)[0].astype(BF)
    hidden = gelu_parts(mm(normed_own, up_ref[...]))[0].astype(BF)
    mixed = stream + mm(hidden, down_ref[...])
    mixed_norm, rstd = layer_norm(mixed)
    mnorm[...] = mixed_norm
    rstdb[...] = jnp.broadcast_to(rstd, (ROWS, 128))
    pred[...] = mm(mixed_norm.astype(BF), proj_ref[...])

    def share(slot):
        c = lax.rem(here.x + FAN[slot], 4)
        for k in range(2):
            at = slice((slot * 2 + k) * 128, (slot * 2 + k + 1) * 128)
            rows = jnp.concatenate(
                [sbuf[k, pl.ds(owner(c, k, b) * 256 + c * 64, 64), :] for b in range(2)],
                axis=0,
            )
            nv = layer_norm(rows.astype(F32))[0].astype(BF)
            nall[at, :] = nv
            value, deriv = gelu_parts(mm(nv, ups_ref[...]))
            hid[at, :] = value.astype(BF)
            slope[at, :] = deriv

    share(0)
    share(1)
    ho.done()
    own_a.wait()
    pack = gather_spread(512, GRP)
    total = gt.whole(here.y)[...].astype(F32)
    for dy in (0, 1, 3, 2):
        group = lax.rem(here.y + dy, 4)
        net.came(arecv.at[group], att.at[pl.ds(0, 4 if dy else 3)])
        wide = jnp.concatenate([att[group * 4 + h] for h in range(4)], axis=1)
        total = total + mm(mm(wide, pack).astype(BF), wout[group])
    target = layer_norm(total)[0].astype(BF).astype(F32)
    masked = mask_ref[pl.ds(here.x, 1), :]
    lives = []
    for b in range(2):
        hit = jnp.where(masked == here.seq * 2 + b, 1.0, 0.0)
        lives.append(jnp.broadcast_to(jnp.max(hit, axis=1, keepdims=True), (BLK, 1)))
    live = jnp.concatenate(lives, axis=0) / float(4 * masked.shape[1])
    grad_pred = ((pred[...] - target) * live).astype(BF)
    grad_norm = mm(grad_pred, proj_ref[...], NT)
    mixed_norm = mnorm[...]
    first_mean = jnp.mean(grad_norm, axis=-1, keepdims=True)
    second_mean = jnp.mean(grad_norm * mixed_norm, axis=-1, keepdims=True)
    grad = (rstdb[:, 0:1] * (grad_norm - first_mean - mixed_norm * second_mean)).astype(BF)
    gm[...] = grad
    gmall[here.k, pl.ds(pl.multiple_of(here.x * 128, 128), 128), :] = grad

    gg = RingGather(net, here, "x", gm, rows_at(gmall.at[here.k], 128), 64, 128, gmall.at[0, pl.ds(0, 384)])
    mg = Mirror(
        net, here, gg, gm, gmall.at[0],
        [((0, 1, 2), gmall.at[0, pl.ds(0, 384)]), ((3,), gmall.at[0, pl.ds(0, 128)])],
    )
    gg.start()
    mg.start([0])
    share(2)
    gg.forward()
    share(3)
    gg.near()
    mg.start([1, 2])
    gg.far()
    mg.start([3])
    mg.wait_recv(0)

    def grads(slots):
        places = [(gg.me, gg.right_pos, gg.left_pos, gg.far_pos)[n] for n in slots]
        rows = [
            gmall[k, pl.ds(pl.multiple_of(pos * 128, 128), 128), :]
            for pos in places for k in range(2)
        ]
        grad_mixed = jnp.concatenate(rows, axis=0)
        at = slice(slots[0] * 256, (slots[-1] + 1) * 256)
        down = mm(hid[at, :], grad_mixed, TN)
        grad_hidden = mm(grad_mixed, pds_ref[...], NT)
        grad_pre = (grad_hidden * slope[at, :]).astype(BF)
        return mm(grad_pre, nall[at, :], TN), down

    up_near, down_near = grads((0, 1, 2))
    mg.wait_recv(1)
    grad_up, grad_down = grads((3,))
    grad_up = grad_up + up_near
    grad_down = grad_down + down_near
    grad_up = grad_up.reshape(16, 2, 8, PD)
    grad_down = grad_down.reshape(16, 2, 8, PD)
    low = lax.broadcasted_iota(jnp.int32, (8, PD), 0) < 4
    part[:, :, 0:PD] = grad_up[:, 0].astype(BF)
    part[:, :, PD:2 * PD] = grad_down[:, 0].astype(BF)
    for d in range(16):
        both = jnp.where(low, grad_up[d, 1], pltpu.roll(grad_down[d, 1], 4, 0))
        part[d, :, 2 * PD:3 * PD] = both.astype(BF)

    me = here.z * 4 + here.y
    for d in range(1, 16):
        to = lax.rem(me + d, 16)
        net.copy(
            part.at[to], land.at[me], here.at(z=lax.div(to, 4), y=lax.rem(to, 4)),
            gsend.at[0], grecv.at[0],
        ).start()
    for c in [gt, gs, ho, gg, ms, mg] + gw + mw:
        c.drain()
    for t in range(3):
        net.sent(head_out[t], outq.at[t, pl.ds(0, 3)])
    net.sent(pass_out, kpack)
    net.sent(asend.at[0], atts.at[pl.ds(0, 15)])
    total = part[me].astype(F32)
    net.came(grecv.at[0], land.at[pl.ds(0, 15)])
    for d in range(1, 16):
        total = total + land[lax.rem(me + d, 16)].astype(F32)
    out_ref[0:8, :] = total[:, 0:2 * PD]
    out_ref[8:12, 0:PD] = total[0:4, 2 * PD:3 * PD]
    out_ref[8:12, PD:2 * PD] = total[4:8, 2 * PD:3 * PD]
    net.sent(gsend.at[0], part.at[pl.ds(0, 15)])


VM = pl.BlockSpec(memory_space=pltpu.VMEM)
ANY = pl.BlockSpec(memory_space=pl.ANY)
DMA = pltpu.SemaphoreType.DMA


def sds(shape, dtype):
    return jax.ShapeDtypeStruct(shape, dtype)


def params(cid):
    return pltpu.CompilerParams(
        collective_id=cid, has_side_effects=True, vmem_limit_bytes=60 * 1024 * 1024
    )


def per_device(
    tokens, qkv_weight, out_weight, mask_blocks, owner_map, pred_stream, pred_up, pred_down,
    pred_proj,
):
    share = pl.pallas_call(
        step_kernel,
        out_shape=sds((12, 2 * PD), F32),
        in_specs=[ANY] * 9,
        out_specs=VM,
        scratch_shapes=[
            pltpu.VMEM((4, 56), jnp.int32), pltpu.SMEM((4, 64), jnp.int32),
            pltpu.VMEM((3, 352, 512), BF), pltpu.VMEM((3, 352, GRP), BF),
            pltpu.VMEM((4, ROWS, PD), BF), pltpu.VMEM((4 * BLK, PD), BF),
            pltpu.VMEM((512, D), BF), pltpu.VMEM((512, D), BF), pltpu.VMEM((3, D, GRP), BF),
            pltpu.VMEM((2, 1024, PD), BF), pltpu.VMEM((3, 4, 128, GRP), BF),
            pltpu.VMEM((4, 128, GRP), BF), pltpu.VMEM((2, 4, 128, GRP), BF),
            pltpu.VMEM((2, 4, 128, GRP), BF),
            pltpu.VMEM((4, 512, 128), BF), pltpu.VMEM((2, 4, 512, 128), BF),
            pltpu.VMEM((2, 4, 512, 128), BF),
            pltpu.VMEM((4, GRP, D), BF), pltpu.VMEM((PD, PH), BF), pltpu.VMEM((PH, PD), BF),
            pltpu.VMEM((PD, D), BF), pltpu.VMEM((4, 512, 128), F32),
            pltpu.VMEM((16, 128, 128), BF), pltpu.VMEM((16, 128, 128), BF),
            pltpu.VMEM((ROWS, D), F32), pltpu.VMEM((ROWS, PD), F32), pltpu.VMEM((ROWS, 128), F32),
            pltpu.VMEM((PD, HS), BF), pltpu.VMEM((HS, PD), BF), pltpu.VMEM((1024, PD), BF),
            pltpu.VMEM((1024, HS), BF), pltpu.VMEM((1024, HS), F32), pltpu.VMEM((ROWS, PD), BF),
            pltpu.VMEM((2, 512, PD), BF), pltpu.VMEM((16, 8, 3 * PD), BF),
            pltpu.VMEM((16, 8, 3 * PD), BF),
            DMA((17,)), DMA((44,)), DMA((1,)), DMA((4,)), DMA((1,)), DMA((1,)), DMA((15,)),
        ],
        compiler_params=params(1),
        name="step",
    )(
        tokens[0], qkv_weight, pred_stream[0], out_weight, pred_up, pred_down, pred_proj,
        mask_blocks, owner_map,
    )
    return share[:, :PD].T, share[:, PD:]


def solution(mesh):
    in_specs = (
        P("batch", "seq", None),
        P("batch", None),
        P("batch", None),
        P(),
        P(),
        P("batch", None, "seq", None),
        P(),
        P(),
        P(),
    )
    out_specs = (P(None, ("seq", "batch")), P(("seq", "batch"), None))
    return jax.shard_map(
        per_device, mesh=mesh, in_specs=in_specs, out_specs=out_specs, check_vma=False
    )
```
